512 devices in a mesh: row: 16 (over y_lo, x, core), col: 8 (over z), seq: 4 (over y_hi).
Axes of the slice: x: 4, y: 8 (y_hi: 4, y_lo: 2; y = y_hi * 2 + y_lo), z: 8, core: 2. Of those that a mesh axis runs over, the one named last changes fastest.
Arguments:
- left_piece: bfloat16 [512, 32, 1024], P('seq', None, 'row'), may hold values from -6 to 6
- right_piece: bfloat16 [512, 32, 1024], P('seq', 'row', 'col'), may hold values from -6 to 6
- proj_weight: bfloat16 [1024, 128], replicated, may hold values from -4 to 4
- proj_bias: float32 [128], replicated, may hold values from -3 to 3
- pair_rep: bfloat16 [1024, 1024, 128], P(('row', 'seq'), 'col'), may hold values from -6 to 6
- norm_gain: float32 [128], replicated, may hold values from 0.5 to 1.5
- up_weight: bfloat16 [128, 512], replicated, may hold values from -0.5 to 0.5
- up_bias: float32 [512], replicated, may hold values from -3 to 3
- down_weight: bfloat16 [512, 128], replicated, may hold values from -0.25 to 0.25
- down_bias: float32 [128], replicated, may hold values from -3 to 3
Outputs:
- refined: bfloat16 [1024, 1024, 128], P(('row', 'seq'), 'col')
The draws below stay inside these ranges and needn't reach their ends.
All inputs are finite; a program needn't handle non-finite values.
Results may differ from the reference program's by a relative error of at most 0.0085.
Values may be sent and summed in bfloat16 or wider, within the bound.
A program may use at most 64 MiB of HBM per device.

```python
import jax
import jax.numpy as jnp
from jax import lax

C = 32
H = 128
F = 512
GROUPS = 4
S = 512
N = 1024


def shard_levels(own_key, shape, pieces, least, largest):
    factor_of, own = 1.0, jax.random.fold_in(own_key, 6)
    for position, blocks in pieces:
        heights = jnp.exp(jax.random.uniform(jax.random.fold_in(own, position), (blocks,), jnp.float32, least / len(pieces), largest / len(pieces)))
        factor_of = factor_of * jnp.repeat(heights, shape[position] // blocks).reshape([-1 if axis == position else 1 for axis in range(len(shape))])
    return factor_of


def centred(stream_key, extent, width, limit, cuts=(), held_as=jnp.bfloat16):
    entries = jax.random.normal(stream_key, extent, jnp.float32) * width
    if len(cuts) > 0:
        entries = shard_levels(stream_key, extent, cuts, -0.22, 0.18) * entries
    return jnp.clip(entries, min=-limit, max=limit).astype(held_as)


def setup_inputs(seed: int = 0) -> dict:
    key_of = jax.random.split(jax.random.key(seed), 11)
    return {
        "left_piece": centred(key_of[0], (S, C, N), 1.0, 6.0, ((0, 4), (2, 16))),
        "right_piece": centred(key_of[1], (S, C, N), 1.0, 6.0, ((0, 4), (1, 16), (2, 8))),
        "proj_weight": centred(key_of[2], (C * C, H), (C * C / S) ** -0.5, 4.0),
        "proj_bias": centred(key_of[3], (H,), 0.5, 3.0, (), jnp.float32),
        "pair_rep": centred(key_of[4], (N, N, H), 1.0, 6.0, ((0, 64), (1, 8))),
        "norm_gain": jnp.clip(jax.random.uniform(key_of[5], (H,), jnp.float32, 0.5, 1.5), 0.5, 1.5),
        "up_weight": centred(key_of[6], (H, F), H ** -0.5, 0.5),
        "up_bias": centred(key_of[7], (F,), 0.5, 3.0, (), jnp.float32),
        "down_weight": centred(key_of[8], (F, H), F ** -0.5, 0.25),
        "down_bias": centred(key_of[9], (H,), 0.5, 3.0, (), jnp.float32),
    }


epsilon = 1e-05

def project_block(row_slab, right_all, proj_weight):
    seq_count, channels, row_count = row_slab.shape
    columns = right_all.shape[2]
    left_mat = row_slab.reshape(seq_count, channels * row_count)
    right_mat = right_all.reshape(seq_count, channels * columns)
    outer_prod = lax.dot_general(left_mat, right_mat, (((0,), (0,)), ((), ())), preferred_element_type=jnp.float32).astype(jnp.bfloat16)
    outer_prod = outer_prod.reshape(channels, row_count, channels, columns).transpose(1, 3, 0, 2)
    outer_prod = outer_prod.reshape(row_count * columns, channels * channels)
    result = jnp.dot(outer_prod, proj_weight, preferred_element_type=jnp.float32)
    return result.reshape(row_count, columns, proj_weight.shape[1])

def transition(middle, norm_gain, up_weight, up_bias, down_weight, down_bias):
    row_count, columns, channels = middle.shape
    values = middle.astype(jnp.float32).reshape(row_count * columns, channels)
    center = lax.optimization_barrier(jnp.mean(values, axis=1, keepdims=True))
    spread = lax.optimization_barrier(jnp.mean(jnp.square(values - center), axis=1, keepdims=True))
    normed = ((values - center) * lax.rsqrt(spread + epsilon) * norm_gain).astype(jnp.bfloat16)
    hidden = jnp.maximum(jnp.dot(normed, up_weight, preferred_element_type=jnp.float32) + up_bias, 0.0).astype(jnp.bfloat16)
    result = values + jnp.dot(hidden, down_weight, preferred_element_type=jnp.float32) + down_bias
    return result.astype(jnp.bfloat16).reshape(row_count, columns, channels)

def reference(left_piece, right_piece, proj_weight, proj_bias, pair_rep, norm_gain, up_weight, up_bias, down_weight, down_bias):
    group_len = S // GROUPS
    row_block = 16
    offsets = (jnp.arange(N // row_block) * row_block).astype(jnp.int32)

    def update_rows(offset):
        summed = jnp.zeros((row_block, N, H), jnp.float32)
        for group_id in range(GROUPS):
            left_group = left_piece[group_id * group_len:(group_id + 1) * group_len]
            right_group = right_piece[group_id * group_len:(group_id + 1) * group_len]
            row_slab = lax.dynamic_slice_in_dim(left_group, offset, row_block, 2)
            summed = summed + project_block(row_slab, right_group, proj_weight)
        return (summed / S + proj_bias).astype(jnp.bfloat16)
    update = lax.map(update_rows, offsets).reshape(N, N, H)
    mirrored_all = jnp.transpose(update, (1, 0, 2))

    def finish_rows(offset):
        own_part = lax.dynamic_slice_in_dim(update, offset, row_block, 0).astype(jnp.float32)
        mirrored = lax.dynamic_slice_in_dim(mirrored_all, offset, row_block, 0).astype(jnp.float32)
        residual = lax.dynamic_slice_in_dim(pair_rep, offset, row_block, 0).astype(jnp.float32)
        middle = (residual + 0.5 * (own_part + mirrored)).astype(jnp.bfloat16)
        return transition(middle, norm_gain, up_weight, up_bias, down_weight, down_bias)
    return lax.map(finish_rows, offsets).reshape(N, N, H)
```

```python
import jax
import jax.numpy as jnp
from jax import lax
from jax.experimental import pallas as pl
from jax.experimental.pallas import tpu as pltpu
from jax.sharding import PartitionSpec as P

epsilon = 1e-05
MESH = pl.DeviceIdType.MESH
NX, NY, NZ = 4, 8, 8


def gather_kernel(
    r_loc, r_own, l_piece, l_own, r_all, l_all, own,
    s_a, g_a, s_b, g_b, s_c, g_c, s_z, g_z, s_self,
    s_rx, g_rx, s_rr, g_rr, s_rl, g_rl, s_rp, g_rp,
    s_lx, g_lx, s_lr, g_lr, s_ll, g_ll, s_lp, g_lp,
):
    r = lax.axis_index("row")
    z = lax.axis_index("col")
    q = lax.axis_index("seq")
    c = lax.rem(r, 2)
    p = lax.div(r, 2)
    x = lax.rem(p, NX)
    y = 2 * q + lax.div(p, NX)

    def dev(xx, yy, cc, zz):
        return {
            "row": (lax.rem(yy, 2) * NX + xx) * 2 + cc,
            "col": zz,
            "seq": lax.div(yy, 2),
        }

    def at(pp, cc, qq, zz):
        return {"row": pp * 2 + cc, "col": zz, "seq": qq}

    partner = dev(x, y, 1 - c, z)
    up = dev(x, lax.rem(y + 1, NY), c, z)
    down = dev(x, lax.rem(y + NY - 1, NY), c, z)
    x_plus = [dev(lax.rem(x + k, NX), y, c, z) for k in range(NX)]
    diagonal = p == z

    def send(src, dst, ssem, rsem, device):
        return pltpu.make_async_remote_copy(
            src_ref=src, dst_ref=dst, send_sem=ssem, recv_sem=rsem,
            device_id=device, device_id_type=MESH,
        )

    def rblk(k, dy):
        xx = lax.rem(x + NX - k, NX)
        yy = lax.rem(y + NY - dy, NY)
        return r_all.at[(lax.rem(yy, 2) * NX + xx) * 2 + c, lax.div(yy, 2)]

    def lblk(k, dy):
        xx = lax.rem(x + NX - k, NX)
        yy = lax.rem(y + NY - dy, NY)
        return l_all.at[(lax.rem(yy, 2) * NX + xx) * 2 + c, lax.div(yy, 2)]

    barrier = pltpu.get_barrier_semaphore()

    def greet(device):
        pl.semaphore_signal(barrier, inc=1, device_id=device, device_id_type=MESH)

    greet(partner)
    greet(up)
    greet(down)
    for k in range(1, NX):
        greet(x_plus[k])

    @pl.loop(1, NZ)
    def _(k):
        greet(at(p, c, q, lax.rem(z + k, NZ)))

    @pl.loop(1, 4)
    def _(k):
        greet(at(p, c, lax.rem(q + k, 4), z))

    @pl.loop(0, 8)
    def _(k):
        cc, qq = lax.div(k, 4), lax.rem(k, 4)

        @pl.when(jnp.logical_not(diagonal & (cc == c) & (qq == q)))
        def _():
            greet(at(z, cc, qq, p))

    pl.semaphore_wait(barrier, 24 - diagonal.astype(jnp.int32))

    def r_up(t, k):
        return send(rblk(k, t), rblk(k, t), s_rr.at[t, k], g_rr.at[t, k], up)

    def r_down(t, k):
        dy = lax.rem(NY - t, NY)
        return send(rblk(k, dy), rblk(k, dy), s_rl.at[t, k], g_rl.at[t, k], down)

    def r_pair(k, dy):
        return send(rblk(k, dy), rblk(k, dy), s_rp.at[dy, k], g_rp.at[dy, k], partner)

    def l_up(t):
        return send(lblk(0, t), lblk(0, t), s_lr.at[t], g_lr.at[t], up)

    def l_down(t):
        dy = lax.rem(NY - t, NY)
        return send(lblk(0, dy), lblk(0, dy), s_ll.at[t], g_ll.at[t], down)

    def l_x(k, dy):
        return send(lblk(0, dy), lblk(0, dy), s_lx.at[dy, k], g_lx.at[dy, k], x_plus[k])

    def l_pair(k, dy):
        return send(lblk(k, dy), lblk(k, dy), s_lp.at[dy, k], g_lp.at[dy, k], partner)

    def got(ref, sem):
        send(ref, ref, s_self.at[0], sem, partner).wait_recv()

    mine_r = rblk(0, 0)

    def a_copy(cc):
        return send(
            l_piece.at[cc], l_all.at[2 * z + cc, q, c], s_a.at[cc], g_a.at[c],
            at(z, cc, q, p),
        )

    def b_copy(k):
        cc, qq = lax.div(k, 4), lax.rem(k, 4)
        lanes = pl.ds(pl.multiple_of(q * 128, 128), 128)
        rows = pl.ds(pl.multiple_of(c * 32, 32), 32)
        return send(
            r_own.at[k], own.at[p, 1, rows, lanes], s_b.at[k], g_b.at[c * 4 + q],
            at(z, cc, qq, p),
        )

    def own_left():
        lanes = pl.ds(pl.multiple_of(q * 128, 128), 128)
        return own.at[z, 0, :, lanes]

    def c_copy(k):
        qq = lax.rem(q + k, 4)
        return send(
            l_own.at[qq], own_left(), s_c.at[k], g_c.at[k], at(p, c, qq, z)
        )

    first_x = [
        send(r_loc, mine_r, s_rx.at[k], g_rx.at[k], x_plus[k]) for k in range(1, NX)
    ]
    first_up = send(r_loc, mine_r, s_rr.at[0, 0], g_rr.at[0, 0], up)
    first_down = send(r_loc, mine_r, s_rl.at[0, 0], g_rl.at[0, 0], down)
    first_pair = send(r_loc, mine_r, s_rp.at[0, 0], g_rp.at[0, 0], partner)

    for cc in range(2):
        to_self = diagonal & (c == cc)

        @pl.when(jnp.logical_not(to_self))
        def _():
            a_copy(cc).start()

        @pl.when(to_self)
        def _():
            pltpu.make_async_copy(
                l_piece.at[cc], l_all.at[2 * z + cc, q, c], g_a.at[c]
            ).start()

    first_up.start()
    first_down.start()
    for k in range(1, NX):
        first_x[k - 1].start()

    @pl.loop(0, 8)
    def _(k):
        cc, qq = lax.div(k, 4), lax.rem(k, 4)
        to_self = diagonal & (cc == c) & (qq == q)

        @pl.when(jnp.logical_not(to_self))
        def _():
            b_copy(k).start()

        @pl.when(to_self)
        def _():
            lanes = pl.ds(pl.multiple_of(q * 128, 128), 128)
            rows = pl.ds(pl.multiple_of(c * 32, 32), 32)
            pltpu.make_async_copy(
                r_own.at[k], own.at[p, 1, rows, lanes], g_b.at[c * 4 + q]
            ).start()

    @pl.loop(1, 4)
    def _(k):
        c_copy(k).start()

    pltpu.make_async_copy(l_own.at[q], own_left(), g_c.at[0]).start()
    first_pair.start()
    self_copy = pltpu.make_async_copy(r_loc, mine_r, s_self.at[1])
    self_copy.start()

    for cc in range(2):
        got(l_all.at[r, q, cc], g_a.at[cc])
    l_up(0).start()
    l_down(0).start()
    for k in range(1, NX):
        l_x(k, 0).start()
    l_pair(0, 0).start()

    @pl.loop(1, NX)
    def _(k):
        got(rblk(k, 0), g_rx.at[k])
        r_up(0, k).start()
        r_down(0, k).start()
        r_pair(k, 0).start()

    @pl.loop(0, 8)
    def _(k):
        cc, qq = lax.div(k, 4), lax.rem(k, 4)
        lanes = pl.ds(pl.multiple_of(qq * 128, 128), 128)
        rows = pl.ds(pl.multiple_of(cc * 32, 32), 32)
        got(own.at[z, 1, rows, lanes], g_b.at[k])

    @pl.loop(0, 4)
    def _(k):
        qq = lax.rem(q + 4 - k, 4)
        lanes = pl.ds(pl.multiple_of(qq * 128, 128), 128)
        got(own.at[z, 0, :, lanes], g_c.at[k])

    def z_copy(k):
        return send(
            own.at[z], own.at[z], s_z.at[k], g_z.at[k], at(p, c, q, lax.rem(z + k, NZ))
        )

    @pl.loop(1, NZ)
    def _(k):
        z_copy(k).start()

    def x_arrivals(dy):
        for k in range(1, NX):
            got(lblk(k, dy), g_lx.at[dy, k])
            l_pair(k, dy).start()

    @pl.loop(1, 5)
    def _(t):
        got(lblk(0, t), g_lr.at[t - 1])

        @pl.when(t < 4)
        def _():
            l_up(t).start()

        for k in range(1, NX):
            l_x(k, t).start()
        l_pair(0, t).start()

        @pl.when(t < 4)
        def _():
            got(lblk(0, NY - t), g_ll.at[t - 1])

            @pl.when(t < 3)
            def _():
                l_down(t).start()

            for k in range(1, NX):
                l_x(k, NY - t).start()
            l_pair(0, NY - t).start()

        @pl.loop(0, NX)
        def _(k):
            got(rblk(k, t), g_rr.at[t - 1, k])

            @pl.when(t < 4)
            def _():
                r_up(t, k).start()

            r_pair(k, t).start()

            @pl.when(t < 4)
            def _():
                got(rblk(k, NY - t), g_rl.at[t - 1, k])

                @pl.when(t < 3)
                def _():
                    r_down(t, k).start()

                r_pair(k, NY - t).start()

        x_arrivals(t - 1)

        @pl.when(t > 1)
        def _():
            x_arrivals(NY + 1 - t)

    x_arrivals(4)

    @pl.loop(1, NZ)
    def _(k):
        zz = lax.rem(z + NZ - k, NZ)
        got(own.at[zz], g_z.at[k])

    def other(ref, k, dy):
        xx = lax.rem(x + NX - k, NX)
        yy = lax.rem(y + NY - dy, NY)
        return ref.at[(lax.rem(yy, 2) * NX + xx) * 2 + 1 - c, lax.div(yy, 2)]

    @pl.loop(0, NY)
    def _(dy):
        for k in range(NX):
            got(other(r_all, k, dy), g_rp.at[dy, k])
            got(other(l_all, k, dy), g_lp.at[dy, k])
            r_pair(k, dy).wait_send()
            l_pair(k, dy).wait_send()
            if k > 0:
                l_x(k, dy).wait_send()

    self_copy.wait()
    for cc in range(2):

        @pl.when(jnp.logical_not(diagonal & (c == cc)))
        def _():
            a_copy(cc).wait_send()

    @pl.loop(0, 8)
    def _(k):
        cc, qq = lax.div(k, 4), lax.rem(k, 4)

        @pl.when(jnp.logical_not(diagonal & (cc == c) & (qq == q)))
        def _():
            b_copy(k).wait_send()

    for k in range(1, 4):
        c_copy(k).wait_send()
        first_x[k - 1].wait_send()

    @pl.loop(1, NZ)
    def _(k):
        z_copy(k).wait_send()

    @pl.loop(0, 4)
    def _(t):
        l_up(t).wait_send()
        for k in range(NX):
            r_up(t, k).wait_send()

    @pl.loop(0, 3)
    def _(t):
        l_down(t).wait_send()
        for k in range(NX):
            r_down(t, k).wait_send()


def gather(r_loc, r_own, l_piece, l_own):
    dma = pltpu.SemaphoreType.DMA
    sems = []
    for shape in (
        (2,), (8,), (4,), (8,), None, (4,), (4, 4), (3, 4), (8, 4),
        (8, 4), (4,), (3,), (8, 4),
    ):
        if shape is None:
            sems.append(dma((2,)))
        else:
            sems.extend([dma(shape), dma(shape)])
    any_spec = pl.BlockSpec(memory_space=pl.ANY)
    return pl.pallas_call(
        gather_kernel,
        out_shape=(
            jax.ShapeDtypeStruct((16, 4, 128, 256), jnp.bfloat16),
            jax.ShapeDtypeStruct((16, 4, 2, 128, 128), jnp.bfloat16),
            jax.ShapeDtypeStruct((8, 2, 64, 512), jnp.bfloat16),
        ),
        in_specs=[any_spec] * 4,
        out_specs=(any_spec,) * 3,
        scratch_shapes=sems,
        compiler_params=pltpu.CompilerParams(collective_id=0, has_side_effects=True),
        name="gather_pieces",
    )(r_loc, r_own, l_piece, l_own)


def compute_kernel(
    r_ref, l_ref, own_ref, wd_ref, wm_ref, pair_ref, bias_ref, gain_ref,
    up_ref, upb_ref, down_ref, downb_ref, out_ref, lhs_l, lhs_r, wide, acc,
):
    step = pl.program_id(0)

    @pl.when(step == 0)
    def _():
        lhs_l[...] = own_ref[:, 0].reshape(512, 512)
        for k in range(4):
            lanes = slice(k * 128, (k + 1) * 128)
            wide[k] = own_ref[:, 1, :, lanes].reshape(512, 128).astype(jnp.float32)
            for i in range(16):
                lhs_r[i * 32 : (i + 1) * 32, lanes] = wide[
                    k, pl.ds(i, 32, stride=16), :
                ].astype(jnp.bfloat16)

    def project(lhs, pieces, weight):
        tiles = []
        for piece in pieces:
            full = jnp.dot(lhs, piece, preferred_element_type=jnp.float32)
            full = full.astype(jnp.bfloat16)
            tiles.append(full[:, :128])
            tiles.append(full[:, 128:])
        stacked = jnp.concatenate(
            [
                jnp.concatenate([tile[i * 32 : (i + 1) * 32] for tile in tiles], axis=0)
                for i in range(16)
            ],
            axis=1,
        )
        return jnp.dot(weight, stacked, preferred_element_type=jnp.float32)

    right = [r_ref[k].reshape(512, 256) for k in range(4)]
    left = []
    for k in range(4):
        low = l_ref[k, :, 0].reshape(512, 128)
        high = l_ref[k, :, 1].reshape(512, 128)
        left.append(
            jnp.concatenate(
                [low[:, :64], high[:, :64], low[:, 64:], high[:, 64:]], axis=1
            )
        )
    total = project(lhs_l[...], right, wd_ref[...]) + project(lhs_r[...], left, wm_ref[...])

    @pl.when(step == 0)
    def _():
        acc[...] = total

    @pl.when(step > 0)
    def _():
        acc[...] += total

    @pl.when(step == 3)
    def _():
        for i in range(16):
            both = acc[:, i * 128 : (i + 1) * 128].T
            middle = (
                pair_ref[i].astype(jnp.float32)
                + both * (0.5 / 512.0)
                + bias_ref[...]
            )
            values = middle.astype(jnp.bfloat16).astype(jnp.float32)
            center = jnp.mean(values, axis=1, keepdims=True)
            spread = jnp.mean(jnp.square(values - center), axis=1, keepdims=True)
            normed = (values - center) * lax.rsqrt(spread + epsilon) * gain_ref[...]
            hidden = jnp.dot(
                normed.astype(jnp.bfloat16), up_ref[...], preferred_element_type=jnp.float32
            )
            hidden = jnp.maximum(hidden + upb_ref[...], 0.0).astype(jnp.bfloat16)
            result = jnp.dot(hidden, down_ref[...], preferred_element_type=jnp.float32)
            out_ref[i] = (values + result + downb_ref[...]).astype(jnp.bfloat16)


def compute(r_all, l_all, own, wd, wm, pair, bias, gain, up, upb, down, downb):
    def whole(shape):
        return pl.BlockSpec(shape, lambda g: (0,) * len(shape))

    return pl.pallas_call(
        compute_kernel,
        out_shape=jax.ShapeDtypeStruct((16, 128, 128), jnp.bfloat16),
        grid=(4,),
        in_specs=[
            pl.BlockSpec((4, 4, 128, 256), lambda g: (g, 0, 0, 0)),
            pl.BlockSpec((4, 4, 2, 128, 128), lambda g: (g, 0, 0, 0, 0)),
            whole((8, 2, 64, 512)),
            pl.BlockSpec((128, 256), lambda g: (0, g)),
            pl.BlockSpec((128, 256), lambda g: (0, g)),
            whole((16, 128, 128)),
            whole((1, 128)),
            whole((1, 128)),
            whole((128, 512)),
            whole((1, 512)),
            whole((512, 128)),
            whole((1, 128)),
        ],
        out_specs=whole((16, 128, 128)),
        scratch_shapes=[
            pltpu.VMEM((512, 512), jnp.bfloat16),
            pltpu.VMEM((512, 512), jnp.bfloat16),
            pltpu.VMEM((4, 512, 128), jnp.float32),
            pltpu.VMEM((128, 2048), jnp.float32),
        ],
        compiler_params=pltpu.CompilerParams(vmem_limit_bytes=56 << 20),
        name="project_and_refine",
    )(r_all, l_all, own, wd, wm, pair, bias, gain, up, upb, down, downb)


def on_device(
    left_piece, right_piece, proj_weight, proj_bias, pair_rep, norm_gain,
    up_weight, up_bias, down_weight, down_bias,
):
    z = lax.axis_index("col")
    r_loc = right_piece.reshape(128, 256)
    r_own = right_piece.reshape(128, 2, 8, 16).transpose(2, 1, 3, 0).reshape(8, 32, 128)
    l_piece = lax.dynamic_slice_in_dim(left_piece, z * 4, 4, 1)
    l_piece = l_piece.reshape(128, 2, 128).transpose(1, 0, 2)
    l_own = lax.dynamic_slice_in_dim(left_piece.reshape(128, 32, 4, 16), z * 2, 2, 3)
    l_own = l_own.transpose(2, 3, 1, 0).reshape(4, 64, 128)
    weight = proj_weight.reshape(32, 32, 128)
    wd = weight.transpose(2, 1, 0).reshape(128, 1024)
    wm = proj_weight.T
    r_all, l_all, own = gather(r_loc, r_own, l_piece, l_own)
    return compute(
        r_all, l_all, own, wd, wm, pair_rep, proj_bias.reshape(1, 128),
        norm_gain.reshape(1, 128), up_weight, up_bias.reshape(1, 512), down_weight,
        down_bias.reshape(1, 128),
    )


def solution(mesh):
    in_specs = (
        P("seq", None, "row"), P("seq", "row", "col"), P(), P(),
        P(("row", "seq"), "col", None), P(), P(), P(), P(), P(),
    )
    out_specs = P(("row", "seq"), "col", None)
    return jax.shard_map(
        on_device, mesh=mesh, in_specs=in_specs, out_specs=out_specs, check_vma=False
    )
```

```python
import jax
import jax.numpy as jnp
from jax import lax
from jax.experimental import pallas as pl
from jax.experimental.pallas import tpu as pltpu
from jax.sharding import PartitionSpec as P

epsilon = 1e-05
MESH = pl.DeviceIdType.MESH
NX, NY, NZ = 4, 8, 8

SEMS = {
    "a": (2,), "b": (8,), "c": (4,), "z": (8,), "rx": (4,), "ru": (4, 4), "rd": (4, 4),
    "rp": (8, 4), "lx": (8, 4), "lu": (4,), "ld": (4,), "lp": (8, 4), "own": (8,),
}


def fused_kernel(
    l_src, r_src, w_src, pair_src, up_src, down_src, bias_ref, gain_ref, upb_ref,
    downb_ref, out_ref, r_all, l_all, own, r_own, lhs_l, lhs_r, wide, w_in, w_wide, wd,
    wm, pair, up_w, down_w, acc, *sems,
):
    names = list(SEMS)
    ssem = dict(zip(names, sems[: len(names)]))
    gsem = dict(zip(names, sems[len(names) :]))
    r = lax.axis_index("row")
    z = lax.axis_index("col")
    q = lax.axis_index("seq")
    c = lax.rem(r, 2)
    p = lax.div(r, 2)
    x = lax.rem(p, NX)
    ylo = lax.div(p, NX)
    y = 2 * q + ylo

    def dev(xx, yy, cc, zz):
        return {
            "row": (lax.rem(yy, 2) * NX + xx) * 2 + cc,
            "col": zz,
            "seq": lax.div(yy, 2),
        }

    def at(pp, cc, qq, zz):
        return {"row": pp * 2 + cc, "col": zz, "seq": qq}

    partner = dev(x, y, 1 - c, z)
    up = dev(x, lax.rem(y + 1, NY), c, z)
    down = dev(x, lax.rem(y + NY - 1, NY), c, z)
    east = dev(lax.rem(x + 1, NX), y, c, z)
    west = dev(lax.rem(x + NX - 1, NX), y, c, z)
    diagonal = p == z

    def send(src, dst, name, index, device, landing=None):
        landing = index if landing is None else landing
        return pltpu.make_async_remote_copy(
            src_ref=src, dst_ref=dst, send_sem=ssem[name].at[index],
            recv_sem=gsem[name].at[landing], device_id=device, device_id_type=MESH,
        )

    def got(ref, name, index):
        pltpu.make_async_remote_copy(
            src_ref=ref, dst_ref=ref, send_sem=ssem["own"].at[0],
            recv_sem=gsem[name].at[index], device_id=partner, device_id_type=MESH,
        ).wait_recv()

    def block(ref, k, dy, cc):
        xx = lax.rem(x + NX - k, NX)
        yy = lax.rem(y + NY - dy, NY)
        return ref.at[(lax.rem(yy, 2) * NX + xx) * 2 + cc, lax.div(yy, 2)]

    def rblk(k, dy):
        return block(r_all, k, dy, c)

    def lblk(k, dy):
        return block(l_all, k, dy, c)

    def rhalf(k, dy, side):
        return rblk(k, dy).at[pl.ds(side * 64, 64)]

    def lhalf(k, dy, side):
        return lblk(k, dy).at[side]

    def lanes_of(qq):
        return pl.ds(pl.multiple_of(qq * 128, 128), 128)

    barrier = pltpu.get_barrier_semaphore()

    def greet(device):
        pl.semaphore_signal(barrier, inc=1, device_id=device, device_id_type=MESH)

    for neighbour in (partner, up, down, east, west):
        greet(neighbour)

    @pl.loop(1, NZ)
    def _(k):
        greet(at(p, c, q, lax.rem(z + k, NZ)))

    @pl.loop(1, 4)
    def _(k):
        greet(at(p, c, lax.rem(q + k, 4), z))

    @pl.loop(0, 8)
    def _(k):
        cc, qq = lax.div(k, 4), lax.rem(k, 4)

        @pl.when(jnp.logical_not(diagonal & (cc == c) & (qq == q)))
        def _():
            greet(at(z, cc, qq, p))

    local = [
        pltpu.make_async_copy(src, dst, gsem["own"].at[i])
        for i, (src, dst) in enumerate(
            ((w_src, w_in), (pair_src, pair), (up_src, up_w), (down_src, down_w))
        )
    ]
    for copy in local:
        copy.start()

    mine = r_all.at[r, q]
    for e in range(2):
        plane = r_src[:, e, :]
        mine[:, e * 128 : (e + 1) * 128] = plane
        turned = plane.T
        for k in range(8):
            r_own[k, e] = turned[k * 16 : (k + 1) * 16]

    pl.semaphore_wait(barrier, 22 + 1 - diagonal.astype(jnp.int32))

    def a_copy(cc):
        return send(
            l_src.at[pl.ds(4 * z + 2 * cc, 2)], l_all.at[2 * z + cc, q, c], "a", cc,
            at(z, cc, q, p), c,
        )

    def b_copy(k):
        cc, qq = lax.div(k, 4), lax.rem(k, 4)
        return send(
            r_own.at[k], own.at[p, 1, pl.ds(2 * c, 2), :, lanes_of(q)], "b", k,
            at(z, cc, qq, p), c * 4 + q,
        )

    def c_source(qq):
        return l_src.at[pl.ds(4 * z, 4), pl.ds(pl.multiple_of(qq * 16, 16), 16)]

    def c_copy(k):
        qq = lax.rem(q + k, 4)
        return send(
            c_source(qq), own.at[z, 0, :, :, lanes_of(q)], "c", k, at(p, c, qq, z)
        )

    def z_copy(k):
        return send(own.at[z], own.at[z], "z", k, at(p, c, q, lax.rem(z + k, NZ)))

    def r_x(k):
        return send(mine, mine, "rx", k, east if k == 1 else west)

    def r_x_half(k):
        part = rhalf(k, 0, 0 if k == 1 else 1)
        return send(part, part, "rx", 2 if k == 1 else 0, east if k == 1 else west)

    def l_x(k, dy):
        return send(lblk(0, dy), lblk(0, dy), "lx", (dy, k), east if k == 1 else west)

    def l_x_half(k, dy):
        part = lhalf(k, dy, 0 if k == 1 else 1)
        slot = 2 if k == 1 else 0
        return send(part, part, "lx", (dy, slot), east if k == 1 else west)

    def r_up(t, k):
        ref = rblk(k, t) if t < 3 else rhalf(k, 3, 0)
        return send(ref, ref, "ru", (t, k), up)

    def r_down(t, k):
        ref = rblk(k, -t % NY) if t < 3 else rhalf(k, 5, 1)
        return send(ref, ref, "rd", (t, k), down)

    def l_up(t):
        ref = lblk(0, t) if t < 3 else lhalf(0, 3, 0)
        return send(ref, ref, "lu", t, up)

    def l_down(t):
        ref = lblk(0, -t % NY) if t < 3 else lhalf(0, 5, 1)
        return send(ref, ref, "ld", t, down)

    def r_pair(k, dy):
        return send(rblk(k, dy), rblk(k, dy), "rp", (dy, k), partner)

    def l_pair(k, dy):
        return send(lblk(k, dy), lblk(k, dy), "lp", (dy, k), partner)

    def is_self(cc, qq):
        return diagonal & (cc == c) & (qq == q)

    for cc in range(2):

        @pl.when(jnp.logical_not(is_self(cc, q)))
        def _():
            a_copy(cc).start()

        @pl.when(is_self(cc, q))
        def _():
            pltpu.make_async_copy(
                l_src.at[pl.ds(4 * z + 2 * cc, 2)], l_all.at[2 * z + cc, q, c],
                gsem["a"].at[c],
            ).start()

    r_x(1).start()
    r_x(3).start()
    r_up(0, 0).start()
    r_down(0, 0).start()

    @pl.loop(0, 8)
    def _(k):
        cc, qq = lax.div(k, 4), lax.rem(k, 4)

        @pl.when(jnp.logical_not(is_self(cc, qq)))
        def _():
            b_copy(k).start()

        @pl.when(is_self(cc, qq))
        def _():
            pltpu.make_async_copy(
                r_own.at[k], own.at[p, 1, pl.ds(2 * c, 2), :, lanes_of(q)],
                gsem["b"].at[c * 4 + q],
            ).start()

    @pl.loop(1, 4)
    def _(k):
        c_copy(k).start()

    pltpu.make_async_copy(
        c_source(q), own.at[z, 0, :, :, lanes_of(q)], gsem["c"].at[0]
    ).start()
    r_pair(0, 0).start()

    def l_arrive(dy):
        l_x(1, dy).start()
        l_x(3, dy).start()
        l_pair(0, dy).start()

    def l_step(t):
        if t < 4:
            got(lblk(0, t), "lu", t - 1)
            l_up(t).start()
            l_arrive(t)
            got(lblk(0, NY - t), "ld", t - 1)
            l_down(t).start()
            l_arrive(NY - t)
        else:
            got(lhalf(0, 4, 0), "lu", 3)
            got(lhalf(0, 4, 1), "ld", 3)
            l_arrive(4)

    def dys(t):
        return (t,) if t in (0, 4) else (t, NY - t)

    def l_sides(t):
        for dy in dys(t):
            for k in (1, 3):
                got(lblk(k, dy), "lx", (dy, k))
                l_x_half(k, dy).start()
                l_pair(k, dy).start()

    def l_far(t):
        for dy in dys(t):
            got(lhalf(2, dy, 0), "lx", (dy, 2))
            got(lhalf(2, dy, 1), "lx", (dy, 0))
            l_pair(2, dy).start()

    def r_step(t, k):
        if t < 4:
            got(rblk(k, t), "ru", (t - 1, k))
            r_up(t, k).start()
            r_pair(k, t).start()
            got(rblk(k, NY - t), "rd", (t - 1, k))
            r_down(t, k).start()
            r_pair(k, NY - t).start()
        else:
            got(rhalf(k, 4, 0), "ru", (3, k))
            got(rhalf(k, 4, 1), "rd", (3, k))
            r_pair(k, 4).start()

    def r_sides():
        for k in (1, 3):
            got(rblk(k, 0), "rx", k)
            r_x_half(k).start()
            r_up(0, k).start()
            r_down(0, k).start()
            r_pair(k, 0).start()

    def r_far():
        got(rhalf(2, 0, 0), "rx", 2)
        got(rhalf(2, 0, 1), "rx", 0)
        r_up(0, 2).start()
        r_down(0, 2).start()
        r_pair(2, 0).start()

    def project(group, lhs, pieces, weight):
        tiles = []
        for full in pieces(lhs):
            full = full.astype(jnp.bfloat16)
            tiles.append(full[:, :128])
            tiles.append(full[:, 128:])
        stacked = jnp.concatenate(
            [
                jnp.concatenate([tile[i * 32 : (i + 1) * 32] for tile in tiles], axis=0)
                for i in range(16)
            ],
            axis=1,
        )
        acc[...] += jnp.dot(weight[group], stacked, preferred_element_type=jnp.float32)

    def direct(yy, cc):
        def pieces(lhs):
            for k in range(NX):
                rhs = r_all[yy * 8 + 2 * k + cc].reshape(512, 256)
                yield jnp.dot(lhs, rhs, preferred_element_type=jnp.float32)

        project(yy * 2 + cc, lhs_l[...], pieces, wd)

    def mirror(yy, cc):
        def pieces(lhs):
            for k in range(NX):
                row = yy * 8 + 2 * k + cc
                rhs = jnp.concatenate(
                    [
                        jnp.concatenate(
                            [
                                l_all[row, qq, side, ch]
                                for ch in range(2)
                                for side in range(2)
                            ],
                            axis=0,
                        )
                        for qq in range(4)
                    ],
                    axis=1,
                )
                yield lax.dot_general(
                    lhs, rhs, (((1,), (1,)), ((), ())), preferred_element_type=jnp.float32
                )

        project(yy * 2 + cc, lhs_r[...], pieces, wm)

    def from_partner(ref, name, parity):
        for dy in range(parity, NY, 2):
            for k in range(NX):
                got(block(ref, k, dy, 1 - c), name, (dy, k))

    def prepare_weights():
        for copy in local:
            copy.wait()
        acc[...] = jnp.zeros_like(acc)
        w_wide[...] = w_in[...].astype(jnp.float32)
        for group in range(4):
            rows = [(group // 2) * 8 + 2 * k + group % 2 for k in range(NX)]
            order = [2 * row + e for row in rows for e in range(2)]
            wd[group] = (
                jnp.concatenate([w_wide[pl.ds(e, 32, stride=32), :] for e in order], axis=0)
                .T.astype(jnp.bfloat16)
            )
            wm[group] = (
                jnp.concatenate([w_wide[e * 32 : (e + 1) * 32, :] for e in order], axis=0)
                .T.astype(jnp.bfloat16)
            )

    def prepare_own():
        for side, lhs in ((0, lhs_l), (1, lhs_r)):
            for k in range(4):
                lanes = slice(k * 128, (k + 1) * 128)
                wide[k] = own[:, side, :, :, lanes].reshape(512, 128).astype(jnp.float32)
                for i in range(16):
                    lhs[i * 32 : (i + 1) * 32, lanes] = wide[
                        k, pl.ds(i, 32, stride=16), :
                    ].astype(jnp.bfloat16)

    for cc in range(2):
        got(l_all.at[r, q, cc], "a", cc)
    l_up(0).start()
    l_down(0).start()
    l_arrive(0)
    r_sides()

    @pl.loop(0, 8)
    def _(k):
        cc, qq = lax.div(k, 4), lax.rem(k, 4)
        got(own.at[z, 1, pl.ds(2 * cc, 2), :, lanes_of(qq)], "b", k)

    @pl.loop(0, 4)
    def _(k):
        qq = lax.rem(q + 4 - k, 4)
        got(own.at[z, 0, :, :, lanes_of(qq)], "c", k)

    @pl.loop(1, NZ)
    def _(k):
        z_copy(k).start()

    r_far()
    l_step(1)
    l_sides(0)
    r_step(1, 0)
    prepare_weights()
    for k in (1, 3):
        r_step(1, k)
    l_step(2)
    l_sides(1)
    l_far(0)
    r_step(1, 2)
    r_step(2, 0)
    l_step(3)
    l_sides(2)
    l_far(1)
    for k in (1, 3):
        r_step(2, k)
    l_step(4)
    l_sides(3)
    l_far(2)
    r_step(2, 2)
    r_step(3, 0)

    @pl.loop(1, NZ)
    def _(k):
        zz = lax.rem(z + NZ - k, NZ)
        got(own.at[zz], "z", k)

    prepare_own()
    l_sides(4)
    l_far(3)
    mirror(1 - ylo, c)
    for k in (1, 3, 2):
        r_step(3, k)
    l_far(4)
    from_partner(l_all, "lp", 1)
    mirror(1 - ylo, 1 - c)
    r_step(4, 0)
    mirror(ylo, c)
    for k in (1, 3, 2):
        r_step(4, k)
    from_partner(l_all, "lp", 0)
    mirror(ylo, 1 - c)
    from_partner(r_all, "rp", 1)
    direct(1 - ylo, c)
    direct(1 - ylo, 1 - c)
    direct(ylo, c)
    from_partner(r_all, "rp", 0)
    direct(ylo, 1 - c)

    for i in range(16):
        both = acc[:, i * 128 : (i + 1) * 128].T
        middle = pair[i].astype(jnp.float32) + both * (0.5 / 512.0) + bias_ref[...]
        values = middle.astype(jnp.bfloat16).astype(jnp.float32)
        center = jnp.mean(values, axis=1, keepdims=True)
        spread = jnp.mean(jnp.square(values - center), axis=1, keepdims=True)
        normed = (values - center) * lax.rsqrt(spread + epsilon) * gain_ref[...]
        hidden = jnp.dot(
            normed.astype(jnp.bfloat16), up_w[...], preferred_element_type=jnp.float32
        )
        hidden = jnp.maximum(hidden + upb_ref[...], 0.0).astype(jnp.bfloat16)
        result = jnp.dot(hidden, down_w[...], preferred_element_type=jnp.float32)
        out_ref[i] = (values + result + downb_ref[...]).astype(jnp.bfloat16)

    for cc in range(2):

        @pl.when(jnp.logical_not(is_self(cc, q)))
        def _():
            a_copy(cc).wait_send()

    @pl.loop(0, 8)
    def _(k):
        @pl.when(jnp.logical_not(is_self(lax.div(k, 4), lax.rem(k, 4))))
        def _():
            b_copy(k).wait_send()

    @pl.loop(1, 4)
    def _(k):
        c_copy(k).wait_send()

    @pl.loop(1, NZ)
    def _(k):
        z_copy(k).wait_send()

    for k in (1, 3):
        r_x(k).wait_send()
        r_x_half(k).wait_send()
    for t in range(4):
        l_up(t).wait_send()
        l_down(t).wait_send()
        for k in range(NX):
            r_up(t, k).wait_send()
            r_down(t, k).wait_send()

    @pl.loop(0, NY)
    def _(dy):
        for k in range(NX):
            r_pair(k, dy).wait_send()
            l_pair(k, dy).wait_send()
        for k in (1, 3):
            l_x(k, dy).wait_send()
            l_x_half(k, dy).wait_send()


def on_device(
    left_piece, right_piece, proj_weight, proj_bias, pair_rep, norm_gain,
    up_weight, up_bias, down_weight, down_bias,
):
    any_spec = pl.BlockSpec(memory_space=pl.ANY)
    near = pl.BlockSpec(memory_space=pltpu.VMEM)
    bf16, f32 = jnp.bfloat16, jnp.float32
    sems = [pltpu.SemaphoreType.DMA(shape) for shape in SEMS.values()]
    return pl.pallas_call(
        fused_kernel,
        out_shape=jax.ShapeDtypeStruct((16, 128, 128), bf16),
        in_specs=[any_spec, near] + [any_spec] * 4 + [near] * 4,
        out_specs=near,
        scratch_shapes=[
            pltpu.VMEM((16, 4, 128, 256), bf16),
            pltpu.VMEM((16, 4, 2, 2, 64, 128), bf16),
            pltpu.VMEM((8, 2, 4, 16, 512), bf16),
            pltpu.VMEM((8, 2, 16, 128), bf16),
            pltpu.VMEM((512, 512), bf16),
            pltpu.VMEM((512, 512), bf16),
            pltpu.VMEM((4, 512, 128), f32),
            pltpu.VMEM((1024, 128), bf16),
            pltpu.VMEM((1024, 128), f32),
            pltpu.VMEM((4, 128, 256), bf16),
            pltpu.VMEM((4, 128, 256), bf16),
            pltpu.VMEM((16, 128, 128), bf16),
            pltpu.VMEM((128, 512), bf16),
            pltpu.VMEM((512, 128), bf16),
            pltpu.VMEM((128, 2048), f32),
        ]
        + sems
        + sems,
        compiler_params=pltpu.CompilerParams(
            collective_id=0, has_side_effects=True, vmem_limit_bytes=56 << 20
        ),
        name="gather_and_refine",
    )(
        left_piece.transpose(1, 2, 0), right_piece, proj_weight, pair_rep, up_weight,
        down_weight, proj_bias.reshape(1, 128), norm_gain.reshape(1, 128),
        up_bias.reshape(1, 512), down_bias.reshape(1, 128),
    )


def solution(mesh):
    in_specs = (
        P("seq", None, "row"), P("seq", "row", "col"), P(), P(),
        P(("row", "seq"), "col", None), P(), P(), P(), P(), P(),
    )
    out_specs = P(("row", "seq"), "col", None)
    return jax.shard_map(
        on_device, mesh=mesh, in_specs=in_specs, out_specs=out_specs, check_vma=False
    )
```

```python
import jax
import jax.numpy as jnp
from jax import lax
from jax.experimental import pallas as pl
from jax.experimental.pallas import tpu as pltpu
from jax.sharding import PartitionSpec as P

epsilon = 1e-05
MESH = pl.DeviceIdType.MESH
NX, NY, NZ = 4, 8, 8

ARRIVALS = {
    "a": (1,), "b": (1,), "c": (1,), "z": (4, 2), "rx": (4,), "r": (4, 4), "rp": (2,),
    "lx": (5, 2), "l": (4,), "lp": (2,), "own": (4,),
}
DEPARTURES = ("a", "b", "c", "z", "r", "l", "near")
LEAVES_BY = {"rp": "r", "lx": "l", "lp": "l", "rx": "near", "l": "near"}


def fused_kernel(
    l_src, r_src, w_src, pair_src, up_src, down_src, bias_ref, gain_ref, upb_ref,
    downb_ref, out_ref, r_all, l_all, own, r_own, lhs_l, lhs_r, wide, w_in, w_wide, wd,
    wm, pair, up_w, down_w, acc, tokens, *sems,
):
    gsem = dict(zip(ARRIVALS, sems))
    ssem = dict(zip(DEPARTURES, (sems[-1].at[i] for i in range(len(DEPARTURES)))))
    r = lax.axis_index("row")
    z = lax.axis_index("col")
    q = lax.axis_index("seq")
    c = lax.rem(r, 2)
    p = lax.div(r, 2)
    x = lax.rem(p, NX)
    ylo = lax.div(p, NX)
    y = 2 * q + ylo

    def dev(xx, yy, cc, zz):
        return {
            "row": (lax.rem(yy, 2) * NX + xx) * 2 + cc,
            "col": zz,
            "seq": lax.div(yy, 2),
        }

    def at(pp, cc, qq, zz):
        return {"row": pp * 2 + cc, "col": zz, "seq": qq}

    partner = dev(x, y, 1 - c, z)
    up = dev(x, lax.rem(y + 1, NY), c, z)
    down = dev(x, lax.rem(y + NY - 1, NY), c, z)
    east = dev(lax.rem(x + 1, NX), y, c, z)
    west = dev(lax.rem(x + NX - 1, NX), y, c, z)
    diagonal = p == z

    def send(src, dst, name, landing, device):
        return pltpu.make_async_remote_copy(
            src_ref=src, dst_ref=dst, send_sem=ssem[LEAVES_BY.get(name, name)],
            recv_sem=gsem[name].at[landing], device_id=device, device_id_type=MESH,
        )

    def got(ref, name, index):
        pltpu.make_async_remote_copy(
            src_ref=ref, dst_ref=ref, send_sem=ssem["a"], recv_sem=gsem[name].at[index],
            device_id=partner, device_id_type=MESH,
        ).wait_recv()

    def left(ref, name):
        pltpu.make_async_remote_copy(
            src_ref=ref, dst_ref=ref, send_sem=ssem[name], recv_sem=gsem["a"].at[0],
            device_id=partner, device_id_type=MESH,
        ).wait_send()

    def block(ref, k, dy, cc):
        xx = lax.rem(x + NX - k, NX)
        yy = lax.rem(y + NY - dy, NY)
        return ref.at[(lax.rem(yy, 2) * NX + xx) * 2 + cc, lax.div(yy, 2)]

    def rblk(k, dy):
        return block(r_all, k, dy, c)

    def lblk(k, dy):
        return block(l_all, k, dy, c)

    def rhalf(k, dy, side):
        return rblk(k, dy).at[pl.ds(side * 64, 64)]

    def lhalf(k, dy, side):
        return lblk(k, dy).at[side]

    def lanes_of(qq):
        return pl.ds(pl.multiple_of(qq * 128, 128), 128)

    barrier = pltpu.get_barrier_semaphore()

    def greet(device):
        pl.semaphore_signal(barrier, inc=1, device_id=device, device_id_type=MESH)

    greet(partner)
    for k in range(1, NX):
        greet(dev(lax.rem(x + k, NX), y, c, z))

    @pl.loop(1, NY)
    def _(k):
        greet(dev(x, lax.rem(y + k, NY), c, z))
        greet(at(p, c, q, lax.rem(z + k, NZ)))

    for cc in range(2):

        @pl.when(jnp.logical_not(diagonal & (c == cc)))
        def _():
            greet(at(z, cc, q, z))

    local = [
        pltpu.make_async_copy(src, dst, gsem["own"].at[i])
        for i, (src, dst) in enumerate(
            ((w_src, w_in), (pair_src, pair), (up_src, up_w), (down_src, down_w))
        )
    ]
    for copy in local:
        copy.start()

    mine = r_all.at[r, q]
    for e in range(2):
        plane = r_src[:, e, :]
        mine[:, e * 128 : (e + 1) * 128] = plane
        turned = plane.T
        for k in range(8):
            r_own[k, e] = turned[k * 16 : (k + 1) * 16]

    def prepare_weights():
        for copy in local:
            copy.wait()
        acc[...] = jnp.zeros_like(acc)
        w_wide[...] = w_in[...].astype(jnp.float32)
        for group in range(4):
            rows = [(group // 2) * 8 + 2 * k + group % 2 for k in range(NX)]
            order = [2 * row + e for row in rows for e in range(2)]
            wd[group] = (
                jnp.concatenate([w_wide[pl.ds(e, 32, stride=32), :] for e in order], axis=0)
                .T.astype(jnp.bfloat16)
            )
            wm[group] = (
                jnp.concatenate([w_wide[e * 32 : (e + 1) * 32, :] for e in order], axis=0)
                .T.astype(jnp.bfloat16)
            )

    prepare_weights()
    pl.semaphore_wait(barrier, 18 + 15 * diagonal.astype(jnp.int32))

    def token(step, device):
        pl.semaphore_signal(tokens.at[step], inc=1, device_id=device, device_id_type=MESH)

    @pl.loop(1, NY)
    def _(k):
        token(0, dev(x, lax.rem(y + k, NY), c, z))

    def a_copy(row):
        return send(
            l_src.at[pl.ds(2 * row, 2)], l_all.at[row, q, c], "a", 0,
            {"row": row, "col": z, "seq": q},
        )

    def b_copy(k):
        cc, qq = lax.div(k, 4), lax.rem(k, 4)
        return send(
            r_own.at[k], own.at[p, 1, pl.ds(2 * c, 2), :, lanes_of(q)], "b", 0,
            at(z, cc, qq, p),
        )

    def c_source(qq):
        return l_src.at[pl.ds(4 * z, 4), pl.ds(pl.multiple_of(qq * 16, 16), 16)]

    def c_copy(k):
        qq = lax.rem(q + k, 4)
        return send(
            c_source(qq), own.at[z, 0, :, :, lanes_of(q)], "c", 0, at(p, c, qq, z)
        )

    def z_block(dz, side):
        return own.at[lax.rem(z + NZ - dz, NZ), side]

    def z_half(dz, side, part):
        return z_block(dz, side).at[pl.ds(2 * part, 2)]

    def z_up(t, side):
        ref = z_block(t, side) if t < 3 else z_half(3, side, 0)
        return send(ref, ref, "z", (t, side), at(p, c, q, lax.rem(z + 1, NZ)))

    def z_down(t, side):
        ref = z_block(-t % NZ, side) if t < 3 else z_half(5, side, 1)
        return send(ref, ref, "z", (t, side), at(p, c, q, lax.rem(z + NZ - 1, NZ)))

    def r_x(k):
        return send(mine, mine, "rx", k, east if k == 1 else west)

    def r_x_half(k):
        part = rhalf(k, 0, 0 if k == 1 else 1)
        return send(part, part, "rx", 2, east if k == 1 else west)

    def ring(dy):
        return min(dy, NY - dy)

    def l_x(k, dy):
        ref = lblk(0, dy)
        return send(ref, ref, "lx", (ring(dy), 0), east if k == 1 else west)

    def l_x_half(k, dy):
        part = lhalf(k, dy, 0 if k == 1 else 1)
        return send(part, part, "lx", (ring(dy), 1), east if k == 1 else west)

    def r_up(t, k):
        ref = rblk(k, t) if t < 3 else rhalf(k, 3, 0)
        return send(ref, ref, "r", (t, k), up)

    def r_down(t, k):
        ref = rblk(k, -t % NY) if t < 3 else rhalf(k, 5, 1)
        return send(ref, ref, "r", (t, k), down)

    def l_up(t):
        ref = lblk(0, t) if t < 3 else lhalf(0, 3, 0)
        return send(ref, ref, "l", t, up)

    def l_down(t):
        ref = lblk(0, -t % NY) if t < 3 else lhalf(0, 5, 1)
        return send(ref, ref, "l", t, down)

    def r_pair(k, dy):
        return send(rblk(k, dy), rblk(k, dy), "rp", dy % 2, partner)

    def l_pair(k, dy):
        return send(lblk(k, dy), lblk(k, dy), "lp", dy % 2, partner)

    def is_self(cc, qq):
        return diagonal & (cc == c) & (qq == q)

    r_up(0, 0).start()
    r_down(0, 0).start()
    r_x(1).start()
    r_x(3).start()

    @pl.when(diagonal)
    def _():
        pltpu.make_async_copy(
            l_src.at[pl.ds(2 * r, 2)], l_all.at[r, q, c], gsem["a"].at[0]
        ).start()

        @pl.loop(1, 16)
        def _(k):
            a_copy(lax.rem(r + k, 16)).start()

    @pl.loop(1, 4)
    def _(k):
        c_copy(k).start()

    pltpu.make_async_copy(
        c_source(q), own.at[z, 0, :, :, lanes_of(q)], gsem["c"].at[0]
    ).start()
    r_pair(0, 0).start()

    def l_arrive(dy):
        l_x(1, dy).start()
        l_x(3, dy).start()
        l_pair(0, dy).start()

    def l_step(t):
        got(l_all.at[0, pl.ds(0, 2 if t < 4 else 1)], "l", t - 1)
        if t < 4:
            l_up(t).start()
            l_down(t).start()
            l_arrive(t)
            l_arrive(NY - t)
        else:
            l_arrive(4)

    def dys(t):
        return (t,) if t in (0, 4) else (t, NY - t)

    def l_sides(t):
        got(l_all.at[0, pl.ds(0, 2 * len(dys(t)))], "lx", (t, 0))
        for dy in dys(t):
            for k in (1, 3):
                l_x_half(k, dy).start()
        for dy in dys(t):
            for k in (1, 3):
                l_pair(k, dy).start()

    def l_far(t):
        got(l_all.at[0, pl.ds(0, len(dys(t)))], "lx", (t, 1))
        for dy in dys(t):
            l_pair(2, dy).start()

    def r_step(t, k):
        got(r_all.at[0, pl.ds(0, 2 if t < 4 else 1)], "r", (t - 1, k))
        if t < 4:
            r_up(t, k).start()
            r_down(t, k).start()
            r_pair(k, t).start()
            r_pair(k, NY - t).start()
        else:
            r_pair(k, 4).start()

    def r_turn(k):
        got(rblk(k, 0), "rx", k)
        if k != 2:
            r_x_half(k).start()
        r_up(0, k).start()
        r_down(0, k).start()
        r_pair(k, 0).start()

    def project(group, lhs, pieces, weight):
        tiles = []
        for full in pieces(lhs):
            full = full.astype(jnp.bfloat16)
            tiles.append(full[:, :128])
            tiles.append(full[:, 128:])
        stacked = jnp.concatenate(
            [
                jnp.concatenate([tile[i * 32 : (i + 1) * 32] for tile in tiles], axis=0)
                for i in range(16)
            ],
            axis=1,
        )
        acc[...] += jnp.dot(weight[group], stacked, preferred_element_type=jnp.float32)

    def direct(yy, cc):
        def pieces(lhs):
            for k in range(NX):
                rhs = r_all[yy * 8 + 2 * k + cc].reshape(512, 256)
                yield jnp.dot(lhs, rhs, preferred_element_type=jnp.float32)

        project(yy * 2 + cc, lhs_l[...], pieces, wd)

    def mirror(yy, cc):
        def pieces(lhs):
            for k in range(NX):
                row = yy * 8 + 2 * k + cc
                rhs = jnp.concatenate(
                    [
                        jnp.concatenate(
                            [
                                l_all[row, qq, side, ch]
                                for ch in range(2)
                                for side in range(2)
                            ],
                            axis=0,
                        )
                        for qq in range(4)
                    ],
                    axis=1,
                )
                yield lax.dot_general(
                    lhs, rhs, (((1,), (1,)), ((), ())), preferred_element_type=jnp.float32
                )

        project(yy * 2 + cc, lhs_r[...], pieces, wm)

    def from_partner(ref, name, parity):
        got(ref.at[pl.ds(0, 4)], name, parity)

    def prepare_own(side, lhs):
        for k in range(4):
            lanes = slice(k * 128, (k + 1) * 128)
            wide[k] = own[:, side, :, :, lanes].reshape(512, 128).astype(jnp.float32)
            for i in range(16):
                lhs[i * 32 : (i + 1) * 32, lanes] = wide[
                    k, pl.ds(i, 32, stride=16), :
                ].astype(jnp.bfloat16)

    def own_left():
        got(own.at[z, 0], "c", 0)
        z_up(0, 0).start()
        z_down(0, 0).start()

    def own_right():
        got(own.at[z, 1], "b", 0)
        z_up(0, 1).start()
        z_down(0, 1).start()

    def z_step(t, side):
        got(own.at[0] if t < 4 else own.at[0, 0], "z", (t - 1, side))
        if t < 4:
            z_up(t, side).start()
            z_down(t, side).start()

    def own_send():
        @pl.loop(0, 8)
        def _(k):
            cc, qq = lax.div(k, 4), lax.rem(k, 4)

            @pl.when(jnp.logical_not(is_self(cc, qq)))
            def _():
                b_copy(k).start()

            @pl.when(is_self(cc, qq))
            def _():
                pltpu.make_async_copy(
                    r_own.at[k], own.at[p, 1, pl.ds(2 * c, 2), :, lanes_of(q)],
                    gsem["b"].at[0],
                ).start()

    r_turn(1)
    r_turn(3)
    pl.semaphore_wait(tokens.at[0], 7)

    @pl.loop(1, NZ)
    def _(k):
        token(1, at(p, c, q, lax.rem(z + k, NZ)))

    got(l_all.at[r, q], "a", 0)
    l_up(0).start()
    l_down(0).start()
    l_arrive(0)
    pl.semaphore_wait(tokens.at[1], 7)
    token(2, partner)
    r_step(1, 0)
    pl.semaphore_wait(tokens.at[2], 1)
    own_send()
    own_left()
    l_step(1)
    r_turn(2)
    r_step(1, 1)
    l_sides(0)
    z_step(1, 0)
    l_step(2)
    r_step(1, 3)
    r_step(1, 2)
    l_far(0)
    z_step(2, 0)
    l_sides(1)
    l_step(3)
    own_right()
    r_step(2, 0)
    r_step(2, 1)
    z_step(3, 0)
    l_far(1)
    l_step(4)
    r_step(2, 3)
    z_step(1, 1)
    l_sides(2)
    r_step(2, 2)
    z_step(4, 0)
    r_step(3, 0)
    z_step(2, 1)
    l_far(2)
    l_sides(3)
    r_step(3, 1)
    r_step(3, 3)
    z_step(3, 1)
    l_sides(4)
    l_far(3)
    r_step(3, 2)
    prepare_own(0, lhs_l)
    direct(1 - ylo, c)
    l_far(4)
    r_step(4, 0)
    from_partner(r_all, "rp", 1)
    direct(1 - ylo, 1 - c)
    r_step(4, 1)
    z_step(4, 1)
    prepare_own(1, lhs_r)
    from_partner(l_all, "lp", 1)
    mirror(1 - ylo, c)
    r_step(4, 3)
    mirror(1 - ylo, 1 - c)
    r_step(4, 2)
    from_partner(l_all, "lp", 0)
    mirror(ylo, c)
    mirror(ylo, 1 - c)
    direct(ylo, c)
    from_partner(r_all, "rp", 0)
    direct(ylo, 1 - c)

    for i in range(16):
        both = acc[:, i * 128 : (i + 1) * 128].T
        middle = pair[i].astype(jnp.float32) + both * (0.5 / 512.0) + bias_ref[...]
        values = middle.astype(jnp.bfloat16).astype(jnp.float32)
        center = jnp.mean(values, axis=1, keepdims=True)
        spread = jnp.mean(jnp.square(values - center), axis=1, keepdims=True)
        normed = (values - center) * lax.rsqrt(spread + epsilon) * gain_ref[...]
        hidden = jnp.dot(
            normed.astype(jnp.bfloat16), up_w[...], preferred_element_type=jnp.float32
        )
        hidden = jnp.maximum(hidden + upb_ref[...], 0.0).astype(jnp.bfloat16)
        result = jnp.dot(hidden, down_w[...], preferred_element_type=jnp.float32)
        out_ref[i] = (values + result + downb_ref[...]).astype(jnp.bfloat16)

    @pl.when(diagonal)
    def _():
        left(l_all.at[pl.ds(0, 15), 0, 0], "a")
        left(r_own.at[pl.ds(0, 7)], "b")

    @pl.when(jnp.logical_not(diagonal))
    def _():
        left(r_own, "b")

    left(own.at[pl.ds(0, 3), 0, :, :, pl.ds(0, 128)], "c")
    left(own.at[pl.ds(0, 7)], "z")
    left(r_all.at[pl.ds(0, 15)], "r")
    left(l_all.at[pl.ds(0, 14)], "l")
    left(l_all.at[pl.ds(0, 10), 0], "near")


def on_device(
    left_piece, right_piece, proj_weight, proj_bias, pair_rep, norm_gain,
    up_weight, up_bias, down_weight, down_bias,
):
    any_spec = pl.BlockSpec(memory_space=pl.ANY)
    near = pl.BlockSpec(memory_space=pltpu.VMEM)
    bf16, f32 = jnp.bfloat16, jnp.float32
    sems = [pltpu.SemaphoreType.DMA(shape) for shape in ARRIVALS.values()]
    return pl.pallas_call(
        fused_kernel,
        out_shape=jax.ShapeDtypeStruct((16, 128, 128), bf16),
        in_specs=[any_spec, near] + [any_spec] * 4 + [near] * 4,
        out_specs=near,
        scratch_shapes=[
            pltpu.VMEM((16, 4, 128, 256), bf16),
            pltpu.VMEM((16, 4, 2, 2, 64, 128), bf16),
            pltpu.VMEM((8, 2, 4, 16, 512), bf16),
            pltpu.VMEM((8, 2, 16, 128), bf16),
            pltpu.VMEM((512, 512), bf16),
            pltpu.VMEM((512, 512), bf16),
            pltpu.VMEM((4, 512, 128), f32),
            pltpu.VMEM((1024, 128), bf16),
            pltpu.VMEM((1024, 128), f32),
            pltpu.VMEM((4, 128, 256), bf16),
            pltpu.VMEM((4, 128, 256), bf16),
            pltpu.VMEM((16, 128, 128), bf16),
            pltpu.VMEM((128, 512), bf16),
            pltpu.VMEM((512, 128), bf16),
            pltpu.VMEM((128, 2048), f32),
            pltpu.SemaphoreType.REGULAR((3,)),
        ]
        + sems
        + [pltpu.SemaphoreType.DMA((len(DEPARTURES),))],
        compiler_params=pltpu.CompilerParams(
            collective_id=0, has_side_effects=True, vmem_limit_bytes=56 << 20
        ),
        name="gather_and_refine",
    )(
        left_piece.transpose(1, 2, 0), right_piece, proj_weight, pair_rep, up_weight,
        down_weight, proj_bias.reshape(1, 128), norm_gain.reshape(1, 128),
        up_bias.reshape(1, 512), down_bias.reshape(1, 128),
    )


def solution(mesh):
    in_specs = (
        P("seq", None, "row"), P("seq", "row", "col"), P(), P(),
        P(("row", "seq"), "col", None), P(), P(), P(), P(), P(),
    )
    out_specs = P(("row", "seq"), "col", None)
    return jax.shard_map(
        on_device, mesh=mesh, in_specs=in_specs, out_specs=out_specs, check_vma=False
    )
```

```python
import jax
import jax.numpy as jnp
from jax import lax
from jax.experimental import pallas as pl
from jax.experimental.pallas import tpu as pltpu
from jax.sharding import PartitionSpec as P

epsilon = 1e-05
MESH = pl.DeviceIdType.MESH
NX, NY, NZ = 4, 8, 8
PARTS = 4

ARRIVALS = {
    "a": (1,), "b": (1,), "c": (1,), "z": (4, 2), "rx": (4,), "r": (4, 4), "rp": (2,),
    "lx": (5, 2), "l": (4,), "lp": (2,), "own": (13,),
}
DEPARTURES = ("a", "b", "c", "z", "r", "l", "near")
LEAVES_BY = {"rp": "r", "lx": "l", "lp": "l", "rx": "near", "l": "near"}


def fused_kernel(
    l_src, r_src, w_src, pair_src, up_src, down_src, bias_src, gain_src, upb_src,
    downb_src, out_ref, r_in, bias_ref, gain_ref, upb_ref, downb_ref, out_buf, r_all, l_all, own, r_own, lhs_l, lhs_r, wide, w_in, w_wide, wd,
    wm, pair, up_w, down_w, acc, tokens, *sems,
):
    gsem = dict(zip(ARRIVALS, sems))
    ssem = dict(zip(DEPARTURES, (sems[-1].at[i] for i in range(len(DEPARTURES)))))
    r = lax.axis_index("row")
    z = lax.axis_index("col")
    q = lax.axis_index("seq")
    c = lax.rem(r, 2)
    p = lax.div(r, 2)
    x = lax.rem(p, NX)
    ylo = lax.div(p, NX)
    y = 2 * q + ylo

    def dev(xx, yy, cc, zz):
        return {
            "row": (lax.rem(yy, 2) * NX + xx) * 2 + cc,
            "col": zz,
            "seq": lax.div(yy, 2),
        }

    def at(pp, cc, qq, zz):
        return {"row": pp * 2 + cc, "col": zz, "seq": qq}

    partner = dev(x, y, 1 - c, z)
    up = dev(x, lax.rem(y + 1, NY), c, z)
    down = dev(x, lax.rem(y + NY - 1, NY), c, z)
    east = dev(lax.rem(x + 1, NX), y, c, z)
    west = dev(lax.rem(x + NX - 1, NX), y, c, z)
    diagonal = p == z

    def send(src, dst, name, landing, device):
        return pltpu.make_async_remote_copy(
            src_ref=src, dst_ref=dst, send_sem=ssem[LEAVES_BY.get(name, name)],
            recv_sem=gsem[name].at[landing], device_id=device, device_id_type=MESH,
        )

    def got(ref, name, index):
        pltpu.make_async_remote_copy(
            src_ref=ref, dst_ref=ref, send_sem=ssem["a"], recv_sem=gsem[name].at[index],
            device_id=partner, device_id_type=MESH,
        ).wait_recv()

    def left(ref, name):
        pltpu.make_async_remote_copy(
            src_ref=ref, dst_ref=ref, send_sem=ssem[name], recv_sem=gsem["a"].at[0],
            device_id=partner, device_id_type=MESH,
        ).wait_send()

    def block(ref, k, dy, cc):
        xx = lax.rem(x + NX - k, NX)
        yy = lax.rem(y + NY - dy, NY)
        return ref.at[(lax.rem(yy, 2) * NX + xx) * 2 + cc, lax.div(yy, 2)]

    def rblk(k, dy):
        return block(r_all, k, dy, c)

    def lblk(k, dy):
        return block(l_all, k, dy, c)

    def rhalf(k, dy, side):
        return rblk(k, dy).at[pl.ds(side * 64, 64)]

    def lhalf(k, dy, side):
        return lblk(k, dy).at[side]

    def lanes_of(qq):
        return pl.ds(pl.multiple_of(qq * 128, 128), 128)

    barrier = pltpu.get_barrier_semaphore()

    def greet(device):
        pl.semaphore_signal(barrier, inc=1, device_id=device, device_id_type=MESH)

    local = [
        pltpu.make_async_copy(src, dst, gsem["own"].at[i])
        for i, (src, dst) in enumerate(
            (
                (w_src, w_in), (pair_src, pair), (up_src, up_w), (down_src, down_w),
                (bias_src, bias_ref), (gain_src, gain_ref), (upb_src, upb_ref),
                (downb_src, downb_ref),
            )
        )
    ]
    first = pltpu.make_async_copy(r_src, r_in, gsem["own"].at[8])
    first.start()

    greet(partner)
    for k in range(1, NX):
        greet(dev(lax.rem(x + k, NX), y, c, z))

    @pl.loop(1, NY)
    def _(k):
        greet(dev(x, lax.rem(y + k, NY), c, z))
        greet(at(p, c, q, lax.rem(z + k, NZ)))

    for cc in range(2):

        @pl.when(jnp.logical_not(diagonal & (c == cc)))
        def _():
            greet(at(z, cc, q, z))

    for copy in local:
        copy.start()

    mine = r_all.at[r, q]
    first.wait()
    for e in range(2):
        mine[:, e * 128 : (e + 1) * 128] = r_in[:, e, :]

    def prepare_right():
        for e in range(2):
            turned = r_in[:, e, :].T
            for k in range(8):
                r_own[k, e] = turned[k * 16 : (k + 1) * 16]

    def prepare_weights():
        for copy in local:
            copy.wait()
        acc[...] = jnp.zeros_like(acc)
        w_wide[...] = w_in[...].astype(jnp.float32)
        for group in range(4):
            rows = [(group // 2) * 8 + 2 * k + group % 2 for k in range(NX)]
            order = [2 * row + e for row in rows for e in range(2)]
            wd[group] = (
                jnp.concatenate([w_wide[pl.ds(e, 32, stride=32), :] for e in order], axis=0)
                .T.astype(jnp.bfloat16)
            )
            wm[group] = (
                jnp.concatenate([w_wide[e * 32 : (e + 1) * 32, :] for e in order], axis=0)
                .T.astype(jnp.bfloat16)
            )

    pl.semaphore_wait(barrier, 18 + 15 * diagonal.astype(jnp.int32))

    def token(step, device):
        pl.semaphore_signal(tokens.at[step], inc=1, device_id=device, device_id_type=MESH)

    @pl.loop(1, NY)
    def _(k):
        token(0, dev(x, lax.rem(y + k, NY), c, z))

    def a_copy(row):
        return send(
            l_src.at[pl.ds(2 * row, 2)], l_all.at[row, q, c], "a", 0,
            {"row": row, "col": z, "seq": q},
        )

    def b_copy(k):
        cc, qq = lax.div(k, 4), lax.rem(k, 4)
        return send(
            r_own.at[k], own.at[p, 1, pl.ds(2 * c, 2), :, lanes_of(q)], "b", 0,
            at(z, cc, qq, p),
        )

    def c_source(qq):
        return l_src.at[pl.ds(4 * z, 4), pl.ds(pl.multiple_of(qq * 16, 16), 16)]

    def c_copy(k):
        qq = lax.rem(q + k, 4)
        return send(
            c_source(qq), own.at[z, 0, :, :, lanes_of(q)], "c", 0, at(p, c, qq, z)
        )

    def z_block(dz, side):
        return own.at[lax.rem(z + NZ - dz, NZ), side]

    def z_half(dz, side, part):
        return z_block(dz, side).at[pl.ds(2 * part, 2)]

    def z_up(t, side):
        ref = z_block(t, side) if t < 3 else z_half(3, side, 0)
        return send(ref, ref, "z", (t, side), at(p, c, q, lax.rem(z + 1, NZ)))

    def z_down(t, side):
        ref = z_block(-t % NZ, side) if t < 3 else z_half(5, side, 1)
        return send(ref, ref, "z", (t, side), at(p, c, q, lax.rem(z + NZ - 1, NZ)))

    def r_x(k):
        return send(mine, mine, "rx", k, east if k == 1 else west)

    def r_x_half(k):
        part = rhalf(k, 0, 0 if k == 1 else 1)
        return send(part, part, "rx", 2, east if k == 1 else west)

    def ring(dy):
        return min(dy, NY - dy)

    def l_x(k, dy):
        ref = lblk(0, dy)
        return send(ref, ref, "lx", (ring(dy), 0), east if k == 1 else west)

    def l_x_half(k, dy):
        part = lhalf(k, dy, 0 if k == 1 else 1)
        return send(part, part, "lx", (ring(dy), 1), east if k == 1 else west)

    def r_up(t, k):
        ref = rblk(k, t) if t < 3 else rhalf(k, 3, 0)
        return send(ref, ref, "r", (t, k), up)

    def r_down(t, k):
        ref = rblk(k, -t % NY) if t < 3 else rhalf(k, 5, 1)
        return send(ref, ref, "r", (t, k), down)

    def l_up(t):
        ref = lblk(0, t) if t < 3 else lhalf(0, 3, 0)
        return send(ref, ref, "l", t, up)

    def l_down(t):
        ref = lblk(0, -t % NY) if t < 3 else lhalf(0, 5, 1)
        return send(ref, ref, "l", t, down)

    def r_pair(k, dy):
        return send(rblk(k, dy), rblk(k, dy), "rp", dy % 2, partner)

    def l_pair(k, dy):
        return send(lblk(k, dy), lblk(k, dy), "lp", dy % 2, partner)

    def is_self(cc, qq):
        return diagonal & (cc == c) & (qq == q)

    r_up(0, 0).start()
    r_down(0, 0).start()
    r_x(1).start()
    r_x(3).start()

    @pl.when(diagonal)
    def _():
        pltpu.make_async_copy(
            l_src.at[pl.ds(2 * r, 2)], l_all.at[r, q, c], gsem["a"].at[0]
        ).start()

        @pl.loop(1, 16)
        def _(k):
            a_copy(lax.rem(r + k, 16)).start()

    @pl.loop(1, 4)
    def _(k):
        c_copy(k).start()

    pltpu.make_async_copy(
        c_source(q), own.at[z, 0, :, :, lanes_of(q)], gsem["c"].at[0]
    ).start()
    r_pair(0, 0).start()

    def l_arrive(dy):
        l_x(1, dy).start()
        l_x(3, dy).start()
        l_pair(0, dy).start()

    def l_step(t):
        got(l_all.at[0, pl.ds(0, 2 if t < 4 else 1)], "l", t - 1)
        if t < 4:
            l_up(t).start()
            l_down(t).start()
            l_arrive(t)
            l_arrive(NY - t)
        else:
            l_arrive(4)

    def dys(t):
        return (t,) if t in (0, 4) else (t, NY - t)

    def l_sides(t):
        got(l_all.at[0, pl.ds(0, 2 * len(dys(t)))], "lx", (t, 0))
        for dy in dys(t):
            for k in (1, 3):
                l_x_half(k, dy).start()
        for dy in dys(t):
            for k in (1, 3):
                l_pair(k, dy).start()

    def l_far(t):
        got(l_all.at[0, pl.ds(0, len(dys(t)))], "lx", (t, 1))
        for dy in dys(t):
            l_pair(2, dy).start()

    def r_step(t, k):
        got(r_all.at[0, pl.ds(0, 2 if t < 4 else 1)], "r", (t - 1, k))
        if t < 4:
            r_up(t, k).start()
            r_down(t, k).start()
            r_pair(k, t).start()
            r_pair(k, NY - t).start()
        else:
            r_pair(k, 4).start()

    def r_turn(k):
        got(rblk(k, 0), "rx", k)
        if k != 2:
            r_x_half(k).start()
        r_up(0, k).start()
        r_down(0, k).start()
        r_pair(k, 0).start()

    def project(group, lhs, pieces, weight):
        tiles = []
        for full in pieces(lhs):
            full = full.astype(jnp.bfloat16)
            tiles.append(full[:, :128])
            tiles.append(full[:, 128:])
        stacked = jnp.concatenate(
            [
                jnp.concatenate([tile[i * 32 : (i + 1) * 32] for tile in tiles], axis=0)
                for i in range(16)
            ],
            axis=1,
        )
        acc[...] += jnp.dot(weight[group], stacked, preferred_element_type=jnp.float32)

    def direct(yy, cc):
        def pieces(lhs):
            for k in range(NX):
                rhs = r_all[yy * 8 + 2 * k + cc].reshape(512, 256)
                yield jnp.dot(lhs, rhs, preferred_element_type=jnp.float32)

        project(yy * 2 + cc, lhs_l[...], pieces, wd)

    def mirror(yy, cc):
        def pieces(lhs):
            for k in range(NX):
                row = yy * 8 + 2 * k + cc
                rhs = jnp.concatenate(
                    [
                        jnp.concatenate(
                            [
                                l_all[row, qq, side, ch]
                                for ch in range(2)
                                for side in range(2)
                            ],
                            axis=0,
                        )
                        for qq in range(4)
                    ],
                    axis=1,
                )
                yield lax.dot_general(
                    lhs, rhs, (((1,), (1,)), ((), ())), preferred_element_type=jnp.float32
                )

        project(yy * 2 + cc, lhs_r[...], pieces, wm)

    def from_partner(ref, name, parity):
        got(ref.at[pl.ds(0, 4)], name, parity)

    def prepare_own(side, lhs):
        for k in range(4):
            lanes = slice(k * 128, (k + 1) * 128)
            wide[k] = own[:, side, :, :, lanes].reshape(512, 128).astype(jnp.float32)
            for i in range(16):
                lhs[i * 32 : (i + 1) * 32, lanes] = wide[
                    k, pl.ds(i, 32, stride=16), :
                ].astype(jnp.bfloat16)

    def own_left():
        got(own.at[z, 0], "c", 0)
        z_up(0, 0).start()
        z_down(0, 0).start()

    def own_right():
        got(own.at[z, 1], "b", 0)
        z_up(0, 1).start()
        z_down(0, 1).start()

    def z_step(t, side):
        got(own.at[0] if t < 4 else own.at[0, 0], "z", (t - 1, side))
        if t < 4:
            z_up(t, side).start()
            z_down(t, side).start()

    def own_send():
        @pl.loop(0, 8)
        def _(k):
            cc, qq = lax.div(k, 4), lax.rem(k, 4)

            @pl.when(jnp.logical_not(is_self(cc, qq)))
            def _():
                b_copy(k).start()

            @pl.when(is_self(cc, qq))
            def _():
                pltpu.make_async_copy(
                    r_own.at[k], own.at[p, 1, pl.ds(2 * c, 2), :, lanes_of(q)],
                    gsem["b"].at[0],
                ).start()

    prepare_right()
    r_turn(1)
    r_turn(3)
    pl.semaphore_wait(tokens.at[0], 7)

    @pl.loop(1, NZ)
    def _(k):
        token(1, at(p, c, q, lax.rem(z + k, NZ)))

    prepare_weights()
    got(l_all.at[r, q], "a", 0)
    l_up(0).start()
    l_down(0).start()
    l_arrive(0)
    pl.semaphore_wait(tokens.at[1], 7)
    token(2, partner)
    r_step(1, 0)
    pl.semaphore_wait(tokens.at[2], 1)
    own_send()
    l_step(1)
    own_left()
    r_turn(2)
    l_sides(0)
    r_step(1, 1)
    l_step(2)
    z_step(1, 0)
    r_step(1, 3)
    r_step(1, 2)
    l_sides(1)
    l_step(3)
    own_right()
    z_step(2, 0)
    r_step(2, 0)
    r_step(2, 1)
    l_sides(2)
    l_step(4)
    r_step(2, 3)
    z_step(1, 1)
    z_step(3, 0)
    r_step(2, 2)
    l_far(0)
    l_sides(3)
    r_step(3, 0)
    z_step(2, 1)
    z_step(4, 0)
    l_sides(4)
    l_far(1)
    r_step(3, 1)
    r_step(3, 3)
    l_far(2)
    prepare_own(0, lhs_l)
    r_step(3, 2)
    z_step(3, 1)
    l_far(3)
    direct(1 - ylo, c)
    l_far(4)
    r_step(4, 0)
    from_partner(r_all, "rp", 1)
    direct(1 - ylo, 1 - c)
    r_step(4, 1)
    z_step(4, 1)
    prepare_own(1, lhs_r)
    from_partner(l_all, "lp", 1)
    mirror(1 - ylo, c)
    r_step(4, 3)
    mirror(1 - ylo, 1 - c)
    r_step(4, 2)
    from_partner(l_all, "lp", 0)
    mirror(ylo, c)
    mirror(ylo, 1 - c)
    direct(ylo, c)
    from_partner(r_all, "rp", 0)
    direct(ylo, 1 - c)

    def out_copy(part):
        span = pl.ds(part * (16 // PARTS), 16 // PARTS)
        return pltpu.make_async_copy(
            out_buf.at[span], out_ref.at[span], gsem["own"].at[9 + part]
        )

    rows = 16 // PARTS
    for part in range(PARTS):
        span = range(part * rows, (part + 1) * rows)
        both = jnp.concatenate([acc[:, i * 128 : (i + 1) * 128].T for i in span], axis=0)
        residual = pair[part * rows : (part + 1) * rows].reshape(rows * 128, 128)
        middle = residual.astype(jnp.float32) + both * (0.5 / 512.0) + bias_ref[...]
        values = middle.astype(jnp.bfloat16).astype(jnp.float32)
        center = jnp.mean(values, axis=1, keepdims=True)
        spread = jnp.mean(jnp.square(values - center), axis=1, keepdims=True)
        normed = (values - center) * lax.rsqrt(spread + epsilon) * gain_ref[...]
        hidden = jnp.dot(
            normed.astype(jnp.bfloat16), up_w[...], preferred_element_type=jnp.float32
        )
        hidden = jnp.maximum(hidden + upb_ref[...], 0.0).astype(jnp.bfloat16)
        result = jnp.dot(hidden, down_w[...], preferred_element_type=jnp.float32)
        result = (values + result + downb_ref[...]).astype(jnp.bfloat16)
        out_buf[part * rows : (part + 1) * rows] = result.reshape(rows, 128, 128)
        out_copy(part).start()

    @pl.when(diagonal)
    def _():
        left(l_all.at[pl.ds(0, 15), 0, 0], "a")
        left(r_own.at[pl.ds(0, 7)], "b")

    @pl.when(jnp.logical_not(diagonal))
    def _():
        left(r_own, "b")

    left(own.at[pl.ds(0, 3), 0, :, :, pl.ds(0, 128)], "c")
    left(own.at[pl.ds(0, 7)], "z")
    left(r_all.at[pl.ds(0, 15)], "r")
    left(l_all.at[pl.ds(0, 14)], "l")
    left(l_all.at[pl.ds(0, 10), 0], "near")
    for part in range(PARTS):
        out_copy(part).wait()


def on_device(
    left_piece, right_piece, proj_weight, proj_bias, pair_rep, norm_gain,
    up_weight, up_bias, down_weight, down_bias,
):
    any_spec = pl.BlockSpec(memory_space=pl.ANY)
    bf16, f32 = jnp.bfloat16, jnp.float32
    sems = [pltpu.SemaphoreType.DMA(shape) for shape in ARRIVALS.values()]
    return pl.pallas_call(
        fused_kernel,
        out_shape=jax.ShapeDtypeStruct((16, 128, 128), bf16),
        in_specs=[any_spec] * 10,
        out_specs=any_spec,
        scratch_shapes=[
            pltpu.VMEM((128, 2, 128), bf16),
            pltpu.VMEM((1, 128), f32),
            pltpu.VMEM((1, 128), f32),
            pltpu.VMEM((1, 512), f32),
            pltpu.VMEM((1, 128), f32),
            pltpu.VMEM((16, 128, 128), bf16),
            pltpu.VMEM((16, 4, 128, 256), bf16),
            pltpu.VMEM((16, 4, 2, 2, 64, 128), bf16),
            pltpu.VMEM((8, 2, 4, 16, 512), bf16),
            pltpu.VMEM((8, 2, 16, 128), bf16),
            pltpu.VMEM((512, 512), bf16),
            pltpu.VMEM((512, 512), bf16),
            pltpu.VMEM((4, 512, 128), f32),
            pltpu.VMEM((1024, 128), bf16),
            pltpu.VMEM((1024, 128), f32),
            pltpu.VMEM((4, 128, 256), bf16),
            pltpu.VMEM((4, 128, 256), bf16),
            pltpu.VMEM((16, 128, 128), bf16),
            pltpu.VMEM((128, 512), bf16),
            pltpu.VMEM((512, 128), bf16),
            pltpu.VMEM((128, 2048), f32),
            pltpu.SemaphoreType.REGULAR((3,)),
        ]
        + sems
        + [pltpu.SemaphoreType.DMA((len(DEPARTURES),))],
        compiler_params=pltpu.CompilerParams(
            collective_id=0, has_side_effects=True, vmem_limit_bytes=56 << 20
        ),
        name="gather_and_refine",
    )(
        left_piece.transpose(1, 2, 0), right_piece, proj_weight, pair_rep, up_weight,
        down_weight, proj_bias.reshape(1, 128), norm_gain.reshape(1, 128),
        up_bias.reshape(1, 512), down_bias.reshape(1, 128),
    )


def solution(mesh):
    in_specs = (
        P("seq", None, "row"), P("seq", "row", "col"), P(), P(),
        P(("row", "seq"), "col", None), P(), P(), P(), P(), P(),
    )
    out_specs = P(("row", "seq"), "col", None)
    return jax.shard_map(
        on_device, mesh=mesh, in_specs=in_specs, out_specs=out_specs, check_vma=False
    )
```

```python
import jax
import jax.numpy as jnp
from jax import lax
from jax.experimental import pallas as pl
from jax.experimental.pallas import tpu as pltpu
from jax.sharding import PartitionSpec as P

epsilon = 1e-05
MESH = pl.DeviceIdType.MESH
NX, NY, NZ = 4, 8, 8
PARTS = 4

ARRIVALS = {
    "a": (1,), "b": (1,), "c": (1,), "z": (4, 2), "rx": (4,), "r": (4, 4), "rp": (2,),
    "lx": (5, 2), "l": (4,), "lp": (2,), "own": (14,),
}
DEPARTURES = ("a", "b", "c", "z", "r", "l", "near")
LEAVES_BY = {"rp": "r", "lx": "l", "lp": "l", "rx": "near", "l": "near"}


def fused_kernel(
    l_src, r_src, w_src, pair_src, up_src, down_src, bias_src, gain_src, upb_src,
    downb_src, out_ref, l_in, r_in, bias_ref, gain_ref, upb_ref, downb_ref, r_all, l_all, own, r_own, lhs_l, lhs_r, wide, w_in, w_wide, wd,
    wm, pair, up_w, down_w, acc, tokens, *sems,
):
    gsem = dict(zip(ARRIVALS, sems))
    ssem = dict(zip(DEPARTURES, (sems[-1].at[i] for i in range(len(DEPARTURES)))))
    r = lax.axis_index("row")
    z = lax.axis_index("col")
    q = lax.axis_index("seq")
    c = lax.rem(r, 2)
    p = lax.div(r, 2)
    x = lax.rem(p, NX)
    ylo = lax.div(p, NX)
    y = 2 * q + ylo

    def dev(xx, yy, cc, zz):
        return {
            "row": (lax.rem(yy, 2) * NX + xx) * 2 + cc,
            "col": zz,
            "seq": lax.div(yy, 2),
        }

    def at(pp, cc, qq, zz):
        return {"row": pp * 2 + cc, "col": zz, "seq": qq}

    partner = dev(x, y, 1 - c, z)
    up = dev(x, lax.rem(y + 1, NY), c, z)
    down = dev(x, lax.rem(y + NY - 1, NY), c, z)
    east = dev(lax.rem(x + 1, NX), y, c, z)
    west = dev(lax.rem(x + NX - 1, NX), y, c, z)
    diagonal = p == z

    def send(src, dst, name, landing, device):
        return pltpu.make_async_remote_copy(
            src_ref=src, dst_ref=dst, send_sem=ssem[LEAVES_BY.get(name, name)],
            recv_sem=gsem[name].at[landing], device_id=device, device_id_type=MESH,
        )

    def got(ref, name, index):
        pltpu.make_async_remote_copy(
            src_ref=ref, dst_ref=ref, send_sem=ssem["a"], recv_sem=gsem[name].at[index],
            device_id=partner, device_id_type=MESH,
        ).wait_recv()

    def left(ref, name):
        pltpu.make_async_remote_copy(
            src_ref=ref, dst_ref=ref, send_sem=ssem[name], recv_sem=gsem["a"].at[0],
            device_id=partner, device_id_type=MESH,
        ).wait_send()

    def block(ref, k, dy, cc):
        xx = lax.rem(x + NX - k, NX)
        yy = lax.rem(y + NY - dy, NY)
        return ref.at[(lax.rem(yy, 2) * NX + xx) * 2 + cc, lax.div(yy, 2)]

    def rblk(k, dy):
        return block(r_all, k, dy, c)

    def lblk(k, dy):
        return block(l_all, k, dy, c)

    def rhalf(k, dy, side):
        return rblk(k, dy).at[pl.ds(side * 64, 64)]

    def lhalf(k, dy, side):
        return lblk(k, dy).at[side]

    def lanes_of(qq):
        return pl.ds(pl.multiple_of(qq * 128, 128), 128)

    barrier = pltpu.get_barrier_semaphore()

    def greet(device):
        pl.semaphore_signal(barrier, inc=1, device_id=device, device_id_type=MESH)

    local = [
        pltpu.make_async_copy(src, dst, gsem["own"].at[i])
        for i, (src, dst) in enumerate(
            (
                (w_src, w_in), (pair_src, pair), (up_src, up_w), (down_src, down_w),
                (bias_src, bias_ref), (gain_src, gain_ref), (upb_src, upb_ref),
                (downb_src, downb_ref),
            )
        )
    ]
    first = pltpu.make_async_copy(r_src, r_in, gsem["own"].at[8])
    first.start()
    second = pltpu.make_async_copy(l_src, l_in, gsem["own"].at[13])
    second.start()

    greet(partner)
    for k in range(1, NX):
        greet(dev(lax.rem(x + k, NX), y, c, z))

    @pl.loop(1, NY)
    def _(k):
        greet(dev(x, lax.rem(y + k, NY), c, z))
        greet(at(p, c, q, lax.rem(z + k, NZ)))

    for cc in range(2):

        @pl.when(jnp.logical_not(diagonal & (c == cc)))
        def _():
            greet(at(z, cc, q, z))

    for copy in local:
        copy.start()

    mine = r_all.at[r, q]
    first.wait()
    second.wait()
    for e in range(2):
        mine[:, e * 128 : (e + 1) * 128] = r_in[:, e, :]

    def prepare_right():
        for e in range(2):
            turned = r_in[:, e, :].T
            for k in range(8):
                r_own[k, e] = turned[k * 16 : (k + 1) * 16]

    def prepare_weights():
        for copy in local:
            copy.wait()
        acc[...] = jnp.zeros_like(acc)
        w_wide[...] = w_in[...].astype(jnp.float32)
        for group in range(4):
            rows = [(group // 2) * 8 + 2 * k + group % 2 for k in range(NX)]
            order = [2 * row + e for row in rows for e in range(2)]
            wd[group] = (
                jnp.concatenate([w_wide[pl.ds(e, 32, stride=32), :] for e in order], axis=0)
                .T.astype(jnp.bfloat16)
            )
            wm[group] = (
                jnp.concatenate([w_wide[e * 32 : (e + 1) * 32, :] for e in order], axis=0)
                .T.astype(jnp.bfloat16)
            )

    pl.semaphore_wait(barrier, 18 + 15 * diagonal.astype(jnp.int32))

    def token(step, device):
        pl.semaphore_signal(tokens.at[step], inc=1, device_id=device, device_id_type=MESH)

    @pl.loop(1, NY)
    def _(k):
        token(0, dev(x, lax.rem(y + k, NY), c, z))

    def a_copy(row):
        return send(
            l_in.at[pl.ds(2 * row, 2)], l_all.at[row, q, c], "a", 0,
            {"row": row, "col": z, "seq": q},
        )

    def b_copy(k):
        cc, qq = lax.div(k, 4), lax.rem(k, 4)
        return send(
            r_own.at[k], own.at[p, 1, pl.ds(2 * c, 2), :, lanes_of(q)], "b", 0,
            at(z, cc, qq, p),
        )

    def c_source(qq):
        return l_in.at[pl.ds(4 * z, 4), pl.ds(pl.multiple_of(qq * 16, 16), 16)]

    def c_copy(k):
        qq = lax.rem(q + k, 4)
        return send(
            c_source(qq), own.at[z, 0, :, :, lanes_of(q)], "c", 0, at(p, c, qq, z)
        )

    def z_block(dz, side):
        return own.at[lax.rem(z + NZ - dz, NZ), side]

    def z_half(dz, side, part):
        return z_block(dz, side).at[pl.ds(2 * part, 2)]

    def z_up(t, side):
        ref = z_block(t, side) if t < 3 else z_half(3, side, 0)
        return send(ref, ref, "z", (t, side), at(p, c, q, lax.rem(z + 1, NZ)))

    def z_down(t, side):
        ref = z_block(-t % NZ, side) if t < 3 else z_half(5, side, 1)
        return send(ref, ref, "z", (t, side), at(p, c, q, lax.rem(z + NZ - 1, NZ)))

    def r_x(k):
        return send(mine, mine, "rx", k, east if k == 1 else west)

    def r_x_half(k):
        part = rhalf(k, 0, 0 if k == 1 else 1)
        return send(part, part, "rx", 2, east if k == 1 else west)

    def ring(dy):
        return min(dy, NY - dy)

    def l_x(k, dy):
        ref = lblk(0, dy)
        return send(ref, ref, "lx", (ring(dy), 0), east if k == 1 else west)

    def l_x_half(k, dy):
        part = lhalf(k, dy, 0 if k == 1 else 1)
        return send(part, part, "lx", (ring(dy), 1), east if k == 1 else west)

    def r_up(t, k):
        ref = rblk(k, t) if t < 3 else rhalf(k, 3, 0)
        return send(ref, ref, "r", (t, k), up)

    def r_down(t, k):
        ref = rblk(k, -t % NY) if t < 3 else rhalf(k, 5, 1)
        return send(ref, ref, "r", (t, k), down)

    def l_up(t):
        ref = lblk(0, t) if t < 3 else lhalf(0, 3, 0)
        return send(ref, ref, "l", t, up)

    def l_down(t):
        ref = lblk(0, -t % NY) if t < 3 else lhalf(0, 5, 1)
        return send(ref, ref, "l", t, down)

    def r_pair(k, dy):
        return send(rblk(k, dy), rblk(k, dy), "rp", dy % 2, partner)

    def l_pair(k, dy):
        return send(lblk(k, dy), lblk(k, dy), "lp", dy % 2, partner)

    def is_self(cc, qq):
        return diagonal & (cc == c) & (qq == q)

    r_up(0, 0).start()
    r_down(0, 0).start()
    r_x(1).start()
    r_x(3).start()

    @pl.when(diagonal)
    def _():
        pltpu.make_async_copy(
            l_in.at[pl.ds(2 * r, 2)], l_all.at[r, q, c], gsem["a"].at[0]
        ).start()

        @pl.loop(1, 16)
        def _(k):
            a_copy(lax.rem(r + k, 16)).start()

    @pl.loop(1, 4)
    def _(k):
        c_copy(k).start()

    pltpu.make_async_copy(
        c_source(q), own.at[z, 0, :, :, lanes_of(q)], gsem["c"].at[0]
    ).start()
    r_pair(0, 0).start()

    def l_arrive(dy):
        l_x(1, dy).start()
        l_x(3, dy).start()
        l_pair(0, dy).start()

    def l_step(t):
        got(l_all.at[0, pl.ds(0, 2 if t < 4 else 1)], "l", t - 1)
        if t < 4:
            l_up(t).start()
            l_down(t).start()
            l_arrive(t)
            l_arrive(NY - t)
        else:
            l_arrive(4)

    def dys(t):
        return (t,) if t in (0, 4) else (t, NY - t)

    def l_sides(t):
        got(l_all.at[0, pl.ds(0, 2 * len(dys(t)))], "lx", (t, 0))
        for dy in dys(t):
            for k in (1, 3):
                l_x_half(k, dy).start()
        for dy in dys(t):
            for k in (1, 3):
                l_pair(k, dy).start()

    def l_far(t):
        got(l_all.at[0, pl.ds(0, len(dys(t)))], "lx", (t, 1))
        for dy in dys(t):
            l_pair(2, dy).start()

    def r_step(t, k):
        got(r_all.at[0, pl.ds(0, 2 if t < 4 else 1)], "r", (t - 1, k))
        if t < 4:
            r_up(t, k).start()
            r_down(t, k).start()
            r_pair(k, t).start()
            r_pair(k, NY - t).start()
        else:
            r_pair(k, 4).start()

    def r_turn(k):
        got(rblk(k, 0), "rx", k)
        if k != 2:
            r_x_half(k).start()
        r_up(0, k).start()
        r_down(0, k).start()
        r_pair(k, 0).start()

    def project(group, lhs, pieces, weight):
        tiles = []
        for full in pieces(lhs):
            full = full.astype(jnp.bfloat16)
            tiles.append(full[:, :128])
            tiles.append(full[:, 128:])
        stacked = jnp.concatenate(
            [
                jnp.concatenate([tile[i * 32 : (i + 1) * 32] for tile in tiles], axis=0)
                for i in range(16)
            ],
            axis=1,
        )
        acc[...] += jnp.dot(weight[group], stacked, preferred_element_type=jnp.float32)

    def direct(yy, cc):
        def pieces(lhs):
            for k in range(NX):
                rhs = r_all[yy * 8 + 2 * k + cc].reshape(512, 256)
                yield jnp.dot(lhs, rhs, preferred_element_type=jnp.float32)

        project(yy * 2 + cc, lhs_l[...], pieces, wd)

    def mirror(yy, cc):
        def pieces(lhs):
            for k in range(NX):
                row = yy * 8 + 2 * k + cc
                rhs = jnp.concatenate(
                    [
                        jnp.concatenate(
                            [
                                l_all[row, qq, side, ch]
                                for ch in range(2)
                                for side in range(2)
                            ],
                            axis=0,
                        )
                        for qq in range(4)
                    ],
                    axis=1,
                )
                yield lax.dot_general(
                    lhs, rhs, (((1,), (1,)), ((), ())), preferred_element_type=jnp.float32
                )

        project(yy * 2 + cc, lhs_r[...], pieces, wm)

    def from_partner(ref, name, parity):
        got(ref.at[pl.ds(0, 4)], name, parity)

    def prepare_own(side, lhs):
        for k in range(4):
            lanes = slice(k * 128, (k + 1) * 128)
            wide[k] = own[:, side, :, :, lanes].reshape(512, 128).astype(jnp.float32)
            for i in range(16):
                lhs[i * 32 : (i + 1) * 32, lanes] = wide[
                    k, pl.ds(i, 32, stride=16), :
                ].astype(jnp.bfloat16)

    def own_left():
        got(own.at[z, 0], "c", 0)
        z_up(0, 0).start()
        z_down(0, 0).start()

    def own_right():
        got(own.at[z, 1], "b", 0)
        z_up(0, 1).start()
        z_down(0, 1).start()

    def z_step(t, side):
        got(own.at[0] if t < 4 else own.at[0, 0], "z", (t - 1, side))
        if t < 4:
            z_up(t, side).start()
            z_down(t, side).start()

    def own_send():
        @pl.loop(0, 8)
        def _(k):
            cc, qq = lax.div(k, 4), lax.rem(k, 4)

            @pl.when(jnp.logical_not(is_self(cc, qq)))
            def _():
                b_copy(k).start()

            @pl.when(is_self(cc, qq))
            def _():
                pltpu.make_async_copy(
                    r_own.at[k], own.at[p, 1, pl.ds(2 * c, 2), :, lanes_of(q)],
                    gsem["b"].at[0],
                ).start()

    prepare_right()
    r_turn(1)
    r_turn(3)
    pl.semaphore_wait(tokens.at[0], 7)

    @pl.loop(1, NZ)
    def _(k):
        token(1, at(p, c, q, lax.rem(z + k, NZ)))

    prepare_weights()
    got(l_all.at[r, q], "a", 0)
    l_up(0).start()
    l_down(0).start()
    l_arrive(0)
    pl.semaphore_wait(tokens.at[1], 7)
    token(2, partner)
    r_step(1, 0)
    pl.semaphore_wait(tokens.at[2], 1)
    own_send()
    l_step(1)
    own_left()
    r_turn(2)
    l_sides(0)
    r_step(1, 1)
    l_step(2)
    own_right()
    r_step(1, 3)
    r_step(1, 2)
    z_step(1, 0)
    l_step(3)
    r_step(2, 0)
    r_step(2, 1)
    l_sides(1)
    z_step(1, 1)
    z_step(2, 0)
    l_step(4)
    r_step(2, 3)
    r_step(2, 2)
    l_sides(2)
    z_step(2, 1)
    z_step(3, 0)
    l_far(0)
    r_step(3, 0)
    l_sides(3)
    z_step(3, 1)
    z_step(4, 0)
    r_step(3, 1)
    r_step(3, 3)
    l_far(1)
    l_sides(4)
    prepare_own(0, lhs_l)
    r_step(3, 2)
    l_far(2)
    l_far(3)
    direct(1 - ylo, c)
    l_far(4)
    r_step(4, 0)
    from_partner(r_all, "rp", 1)
    direct(1 - ylo, 1 - c)
    r_step(4, 1)
    z_step(4, 1)
    prepare_own(1, lhs_r)
    from_partner(l_all, "lp", 1)
    mirror(1 - ylo, c)
    r_step(4, 3)
    mirror(1 - ylo, 1 - c)
    r_step(4, 2)
    from_partner(l_all, "lp", 0)
    mirror(ylo, c)
    mirror(ylo, 1 - c)
    direct(ylo, c)
    from_partner(r_all, "rp", 0)
    direct(ylo, 1 - c)

    rows = 16 // PARTS
    for part in range(PARTS):
        span = range(part * rows, (part + 1) * rows)
        both = jnp.concatenate([acc[:, i * 128 : (i + 1) * 128].T for i in span], axis=0)
        residual = pair[part * rows : (part + 1) * rows].reshape(rows * 128, 128)
        middle = residual.astype(jnp.float32) + both * (0.5 / 512.0) + bias_ref[...]
        values = middle.astype(jnp.bfloat16).astype(jnp.float32)
        center = jnp.mean(values, axis=1, keepdims=True)
        spread = jnp.mean(jnp.square(values - center), axis=1, keepdims=True)
        normed = (values - center) * lax.rsqrt(spread + epsilon) * gain_ref[...]
        hidden = jnp.dot(
            normed.astype(jnp.bfloat16), up_w[...], preferred_element_type=jnp.float32
        )
        hidden = jnp.maximum(hidden + upb_ref[...], 0.0).astype(jnp.bfloat16)
        result = jnp.dot(hidden, down_w[...], preferred_element_type=jnp.float32)
        result = (values + result + downb_ref[...]).astype(jnp.bfloat16)
        out_ref[part * rows : (part + 1) * rows] = result.reshape(rows, 128, 128)

    @pl.when(diagonal)
    def _():
        left(l_all.at[pl.ds(0, 15), 0, 0], "a")
        left(r_own.at[pl.ds(0, 7)], "b")

    @pl.when(jnp.logical_not(diagonal))
    def _():
        left(r_own, "b")

    left(own.at[pl.ds(0, 3), 0, :, :, pl.ds(0, 128)], "c")
    left(own.at[pl.ds(0, 7)], "z")
    left(r_all.at[pl.ds(0, 15)], "r")
    left(l_all.at[pl.ds(0, 14)], "l")
    left(l_all.at[pl.ds(0, 10), 0], "near")


def on_device(
    left_piece, right_piece, proj_weight, proj_bias, pair_rep, norm_gain,
    up_weight, up_bias, down_weight, down_bias,
):
    bf16, f32 = jnp.bfloat16, jnp.float32
    sems = [pltpu.SemaphoreType.DMA(shape) for shape in ARRIVALS.values()]
    return pl.pallas_call(
        fused_kernel,
        out_shape=jax.ShapeDtypeStruct((16, 128, 128), bf16),
        in_specs=[pl.BlockSpec(memory_space=pltpu.HBM)] * 10,
        out_specs=pl.BlockSpec(memory_space=pltpu.VMEM),
        scratch_shapes=[
            pltpu.VMEM((32, 64, 128), bf16),
            pltpu.VMEM((128, 2, 128), bf16),
            pltpu.VMEM((1, 128), f32),
            pltpu.VMEM((1, 128), f32),
            pltpu.VMEM((1, 512), f32),
            pltpu.VMEM((1, 128), f32),
            pltpu.VMEM((16, 4, 128, 256), bf16),
            pltpu.VMEM((16, 4, 2, 2, 64, 128), bf16),
            pltpu.VMEM((8, 2, 4, 16, 512), bf16),
            pltpu.VMEM((8, 2, 16, 128), bf16),
            pltpu.VMEM((512, 512), bf16),
            pltpu.VMEM((512, 512), bf16),
            pltpu.VMEM((4, 512, 128), f32),
            pltpu.VMEM((1024, 128), bf16),
            pltpu.VMEM((1024, 128), f32),
            pltpu.VMEM((4, 128, 256), bf16),
            pltpu.VMEM((4, 128, 256), bf16),
            pltpu.VMEM((16, 128, 128), bf16),
            pltpu.VMEM((128, 512), bf16),
            pltpu.VMEM((512, 128), bf16),
            pltpu.VMEM((128, 2048), f32),
            pltpu.SemaphoreType.REGULAR((3,)),
        ]
        + sems
        + [pltpu.SemaphoreType.DMA((len(DEPARTURES),))],
        compiler_params=pltpu.CompilerParams(
            collective_id=0, has_side_effects=True, vmem_limit_bytes=32 << 20
        ),
        name="gather_and_refine",
    )(
        *(
            pltpu.with_memory_space_constraint(array, pltpu.HBM)
            for array in (        left_piece.transpose(1, 2, 0), right_piece, proj_weight, pair_rep, up_weight,
        down_weight, proj_bias.reshape(1, 128), norm_gain.reshape(1, 128),
        up_bias.reshape(1, 512), down_bias.reshape(1, 128),
            )
        )
    )


def solution(mesh):
    in_specs = (
        P("seq", None, "row"), P("seq", "row", "col"), P(), P(),
        P(("row", "seq"), "col", None), P(), P(), P(), P(), P(),
    )
    out_specs = P(("row", "seq"), "col", None)
    return jax.shard_map(
        on_device, mesh=mesh, in_specs=in_specs, out_specs=out_specs, check_vma=False
    )
```
